512 devices in a mesh: col: 128 (over z, y, core), row: 4 (over x).
Axes of the slice: x: 4, y: 8, z: 8, core: 2. Of those that a mesh axis runs over, the one named last changes fastest.
Arguments:
- panel: int32 [128], replicated, may hold values from 0 to 127, each once
- centres_cols: bfloat16 [65536, 1024], P('col'), may hold values from -1 to 1
- centres_rows: bfloat16 [2048, 1024], P(('row', 'col')), may hold values from -1 to 1
- diag_inverse: float32 [65536, 512], P('col'), as said below
- trailing: float32 [2048, 65536], P('row', 'col'), may hold values from -6 to 6
Outputs:
- updated: float32 [2048, 65536], P('row', 'col')
The draws below stay inside these ranges and needn't reach their ends.
Inputs may be any that keep to these rules, and one draw needn't show every extreme that they name: panel holds each of 0 to 127 once. Each 512 x 512 block of diag_inverse is lower triangular with a positive diagonal.
All inputs are finite; a program needn't handle non-finite values.
Results may differ from the reference program's by a relative error of at most 0.0003.
Values may be sent and summed in bfloat16 or wider, within the bound.
No kernel may reach another device: no remote copies, remote signals or barrier semaphores. Data moves between devices by JAX's collectives and lax.ppermute only.
A program may use at most 64 MiB of HBM per device.

```python
import math
import jax
import jax.numpy as jnp
from jax import lax

D = 1024
BLK = 512
LAYERS = 3
ROWS = 2048
BLOCKS = 128
COLS = 65536
RANK = 32


def centre_law(key, total, salt):
    shared = jax.random.fold_in(key, 7)
    key_mean, key_cent, key_weight = jax.random.split(shared, 3)
    clusters = max(BLK // 4, 4)
    mean_dir = jax.random.normal(key_mean, (D,), jnp.float32)
    centroids = jax.random.normal(key_cent, (clusters, D), jnp.float32)
    weights = jax.random.uniform(key_weight, (clusters,), jnp.float32, 0.5, 1.5)
    own_key = jax.random.fold_in(key, salt)
    key_assign, key_jitter, key_scale = jax.random.split(own_key, 3)
    member = jax.random.randint(key_assign, (total,), 0, clusters)
    jitter = jax.random.normal(key_jitter, (total, D), jnp.float32)
    row_scale = jnp.exp(jax.random.uniform(key_scale, (total,), jnp.float32, -0.6931472, 0.6931472))
    values = weights[member][:, None] * mean_dir[None, :] + 0.7 * centroids[member] + 0.45 * jitter
    values = values * (row_scale / jnp.sqrt(jnp.float32(D)))[:, None]
    return jnp.clip(values, -1.0, 1.0).astype(jnp.bfloat16)


def draw_centres_cols(key, part):
    return centre_law(key, COLS, 1)


def draw_centres_rows(key, part):
    return centre_law(key, ROWS, 2)


def draw_diag_inverse(key, part):
    key_off, key_diag = jax.random.split(key)
    blocks_all = COLS // BLK
    off_diag = jax.random.normal(key_off, (blocks_all, BLK, BLK), jnp.float32) * 0.05
    diag_vals = jax.random.uniform(key_diag, (blocks_all, BLK), jnp.float32, 1.0, 2.0)
    identity = jnp.eye(BLK, dtype=jnp.float32)
    lower = jnp.tril(off_diag, -1) + diag_vals[:, :, None] * identity[None, :, :]
    return (lower / jnp.sqrt(jnp.float32(BLK))).reshape(COLS, BLK)


def levels(stream_key, dims, shards, smallest, top_value):
    def one(position, parts):
        heights = jax.random.uniform(jax.random.fold_in(jax.random.fold_in(stream_key, 6), position), (parts,), jnp.float32, smallest / len(shards), top_value / len(shards))
        return jnp.repeat(jnp.exp(heights), dims[position] // parts).reshape((-1,) + (1,) * (len(dims) - position - 1))

    gain = one(*shards[0])
    for cut in shards[1:]:
        gain = gain * one(*cut)
    return gain


def scatter_about(rng, shape, scale, most, pieces=(), kind=jnp.bfloat16):
    loudness = levels(rng, shape, pieces, -0.22, 0.18) if pieces else 1.0
    drawn = jax.random.normal(rng, shape, jnp.float32) * scale * loudness
    return jnp.minimum(jnp.maximum(drawn, -most), most).astype(kind)


def setup_inputs(seed: int = 0) -> dict:
    keys = jax.random.split(jax.random.key(seed), 6)
    return {
        "panel": jax.random.permutation(keys[0], BLOCKS).astype(jnp.int32),
        "centres_cols": draw_centres_cols(jax.random.fold_in(keys[5], 71), 0),
        "centres_rows": draw_centres_rows(jax.random.fold_in(keys[5], 71), 0),
        "diag_inverse": draw_diag_inverse(jax.random.fold_in(keys[5], 71), 0),
        "trailing": scatter_about(keys[4], (ROWS, COLS), 1.0, 6.0, ((0, 4), (1, 128)), jnp.float32),
    }


def kernel(left, right):
    gram = lax.dot_general(left, right, (((1,), (1,)), ((), ())), preferred_element_type=jnp.float32)
    left_f = left.astype(jnp.float32)
    right_f = right.astype(jnp.float32)
    inv_left = 1.0 / jnp.sqrt(lax.optimization_barrier(jnp.sum(left_f * left_f, axis=1)) + 1e-06)
    inv_right = 1.0 / jnp.sqrt(lax.optimization_barrier(jnp.sum(right_f * right_f, axis=1)) + 1e-06)
    cosine = gram * inv_left[:, None] * inv_right[None, :]
    theta = cosine
    rho_now = cosine
    for layer in range(LAYERS):
        angle_now = jnp.arccos(rho_now)
        zero_order = (math.pi - angle_now) / math.pi
        rho_next = (jnp.sqrt(1.0 - rho_now * rho_now) + (math.pi - angle_now) * rho_now) / math.pi
        theta = theta * zero_order + rho_next
        rho_now = rho_next
    return theta / (inv_left[:, None] * inv_right[None, :])

def apply_inverse(values, inverse):
    return lax.dot_general(values, inverse, (((1,), (1,)), ((), ())), precision=lax.Precision.HIGHEST, preferred_element_type=jnp.float32)

def reference(panel, centres_cols, centres_rows, diag_inverse, trailing):
    block_ids = jnp.arange(BLOCKS, dtype=jnp.int32)
    panel_at = jnp.sum(jnp.where(panel == RANK, block_ids, 0)).astype(jnp.int32)
    start = (panel_at * BLK).astype(jnp.int32)
    panel_x = lax.dynamic_slice_in_dim(centres_cols, start, BLK, 0)
    panel_inv = lax.dynamic_slice_in_dim(diag_inverse, start, BLK, 0)
    rows_l = apply_inverse(kernel(centres_rows, panel_x), panel_inv)
    cols_l = apply_inverse(kernel(centres_cols, panel_x), panel_inv)
    update = lax.dot_general(rows_l, cols_l, (((1,), (1,)), ((), ())), precision=lax.Precision.HIGHEST, preferred_element_type=jnp.float32)
    later = jnp.repeat(panel > RANK, BLK)
    return jnp.where(later[None, :], trailing - update, trailing)
```

```python
import math

import jax
import jax.numpy as jnp
from jax import lax
from jax.sharding import Mesh, PartitionSpec as P

LAYERS = 3
CORES = 2


def repeat_gather(piece, axis, count):
    return lax.all_to_all(jnp.broadcast_to(piece[None], (count,) + piece.shape), axis, 0, 0)


def split(values):
    high = lax.reduce_precision(values, 8, 7)
    return high.astype(jnp.bfloat16), (values - high).astype(jnp.bfloat16)


def dot_t(left, right):
    return lax.dot_general(left, right, (((1,), (1,)), ((), ())), preferred_element_type=jnp.float32)


def dot_pair(left, right):
    return dot_t(left[0], right[0]) + (dot_t(left[0], right[1]) + dot_t(left[1], right[0]))


def norms(pieces):
    total = 0.0
    for piece in pieces:
        wide = piece.astype(jnp.float32)
        total = total + jnp.sum(wide * wide, axis=1)
    return jnp.sqrt(total + 1e-06)


def kernel(left, right):
    gram = sum(dot_t(a, b) for a, b in zip(left, right))
    norm_left, norm_right = norms(left)[:, None], norms(right)[None, :]
    rho = jnp.clip(gram * (1.0 / norm_left) * (1.0 / norm_right), -1.0, 1.0)
    theta = rho
    for layer in range(LAYERS):
        angle = jnp.arccos(rho)
        zero_order = (math.pi - angle) / math.pi
        rho_next = (jnp.sqrt(1.0 - rho * rho) + (math.pi - angle) * rho) / math.pi
        theta = theta * zero_order + rho_next
        rho = rho_next
    return theta * (norm_left * norm_right)


def lanes_first(block):
    return jnp.concatenate([block[:, 128 * i : 128 * (i + 1)] for i in range(block.shape[1] // 128)], axis=0)


def on_device(chips, row_count, panel, centres_cols, centres_rows, diag_inverse, trailing):
    size, width = centres_cols.shape
    blocks = panel.shape[0]
    target_rank = blocks // 4
    half = width // CORES
    quarter = size // row_count
    own_rows = centres_rows.shape[0]
    panel_at = jnp.sum(jnp.where(panel == target_rank, jnp.arange(blocks, dtype=jnp.int32), 0))
    owner_chip, owner_core = panel_at // CORES, panel_at % CORES
    chip, core, row = lax.axis_index("chip"), lax.axis_index("core"), lax.axis_index("row")
    swap = [(0, 1), (1, 0)]

    def share(which):
        x = lax.dynamic_slice(centres_cols, (row * quarter, which * half), (quarter, half))
        inv = lax.dynamic_slice_in_dim(diag_inverse, row * quarter + which * (quarter // CORES), quarter // CORES, 0)
        high, low = split(inv)
        mine = lax.dynamic_slice_in_dim(centres_rows, which * half, half, 1)
        return jnp.concatenate([lanes_first(x), lanes_first(high), lanes_first(low)], axis=0), mine

    kept, rows_kept = share(core)
    sent, rows_sent = share(1 - core)
    n_panel = kept.shape[0]
    swapped = lax.ppermute(jnp.concatenate([sent, lanes_first(rows_sent)], axis=0), "core", swap)
    taken = jnp.where(core == owner_core, kept, swapped[:n_panel])
    groups = half // 128
    rows_got = swapped[n_panel:].reshape(groups, own_rows, 128)
    rows_own = lanes_first(rows_kept).reshape(groups, own_rows, 128)
    first = core == 0
    rows_chip = jnp.concatenate(
        [jnp.where(first, rows_own, rows_got), jnp.where(first, rows_got, rows_own)], axis=1
    ).reshape(groups * CORES * own_rows, 128)

    per_chip = n_panel // chips
    outgoing = jnp.concatenate(
        [taken.reshape(chips, per_chip, 128), jnp.broadcast_to(rows_chip[None], (chips,) + rows_chip.shape)], axis=1
    )
    incoming = lax.all_to_all(outgoing, "chip", 0, 0)
    piece = lax.dynamic_index_in_dim(incoming, owner_chip, 0, keepdims=False)[:per_chip]
    rows_half = incoming[:, per_chip:].reshape(chips, groups, CORES * own_rows, 128)
    rows_half = rows_half.transpose(0, 2, 1, 3).reshape(chips * CORES * own_rows, half)
    rows_other = lax.ppermute(rows_half, "core", swap)

    mine = repeat_gather(piece, "chip", chips).reshape(n_panel, 128)
    all_mine = repeat_gather(mine, "row", row_count)
    all_other = lax.ppermute(all_mine, "core", swap)

    def unpack(got):
        n_x = quarter * groups
        x = got[:, :n_x].reshape(row_count, groups, quarter, 128)
        x = x.transpose(0, 2, 1, 3).reshape(size, half)
        inv = got[:, n_x:].reshape(row_count, 2, size // 128, quarter // CORES, 128)
        inv = inv.transpose(1, 0, 3, 2, 4).reshape(2, size // CORES, size)
        return x, inv

    x_own, inv_own = unpack(all_mine)
    x_other, inv_other = unpack(all_other)
    panel_x = (x_own, x_other)
    cols = (
        lax.dynamic_slice_in_dim(centres_cols, core * half, half, 1),
        lax.dynamic_slice_in_dim(centres_cols, (1 - core) * half, half, 1),
    )
    inverse = [jnp.concatenate([inv_own[i], inv_other[i]], axis=0) for i in range(2)]
    rows_l = dot_pair(split(kernel((rows_half, rows_other), panel_x)), inverse)
    cols_l = dot_pair(split(kernel(cols, panel_x)), inverse)
    update = dot_pair(split(rows_l), split(cols_l))
    own_rank = lax.dynamic_index_in_dim(panel, chip * CORES + core, 0, keepdims=False)
    return jnp.where(own_rank > target_rank, trailing - update, trailing)


def solution(mesh):
    col_count, row_count = mesh.devices.shape
    chips = col_count // CORES
    fine = Mesh(mesh.devices.reshape(chips, CORES, row_count), ("chip", "core", "row"))

    def step(*arrays):
        return on_device(chips, row_count, *arrays)

    col = ("chip", "core")
    return jax.shard_map(
        step,
        mesh=fine,
        in_specs=(P(), P(col, None), P(("row",) + col, None), P(col, None), P("row", col)),
        out_specs=P("row", col),
        check_vma=False,
    )
```

```python
import math

import jax
import jax.numpy as jnp
from jax import lax
from jax.experimental import pallas as pl
from jax.experimental.pallas import tpu as pltpu
from jax.sharding import Mesh, PartitionSpec as P

LAYERS = 3
CORES = 2
LANES = 128
STEP = 128
WIDE = (0.4999999720071538, -0.06830646500676399, 0.028277340639243406, -0.01566003030791659,
        0.008837209300279753, -0.003820798788545866, 0.0008313362870811599)
NARROW = (0.4999769000530011, -0.06803611787881512, 0.026989768593852003, -0.012483028758839653,
          0.004564983607401579, -0.0008544733222650566)


def repeat_gather(piece, axis, count):
    return lax.all_to_all(jnp.broadcast_to(piece[None], (count,) + piece.shape), axis, 0, 0)


def split(values):
    high = values.astype(jnp.bfloat16)
    return high, (values - high.astype(jnp.float32)).astype(jnp.bfloat16)


def dot_t(left, right):
    return lax.dot_general(left, right, (((1,), (1,)), ((), ())), preferred_element_type=jnp.float32)


def root(x):
    return x * lax.rsqrt(jnp.maximum(x, 1e-30))


def arccos_over_pi(x, coefs):
    total = coefs[-1]
    for coef in coefs[-2::-1]:
        total = total * x + coef
    return root(1.0 - x) * total


def layers(rho):
    theta = rho
    for layer in range(LAYERS):
        if layer == 0:
            angle = arccos_over_pi(jnp.abs(rho), WIDE)
            zero_order = jnp.where(rho < 0.0, angle, 1.0 - angle)
        else:
            zero_order = 1.0 - arccos_over_pi(rho, WIDE if layer == 1 else NARROW)
        first_order = root((1.0 - rho) * (1.0 + rho)) * (1.0 / math.pi) + zero_order * rho
        theta = theta * zero_order + first_order
        rho = jnp.minimum(first_order, 1.0)
    return theta


def prep_body(at_ref, x_ref, inv_ref, kept_ref, sent_ref):
    size, half = x_ref.shape[0], x_ref.shape[1] // CORES
    rows = inv_ref.shape[0] // CORES
    core = at_ref[1]
    for out_ref, which in ((kept_ref, core), (sent_ref, 1 - core)):
        for i in range(half // LANES):
            at = pl.multiple_of(which * half + LANES * i, LANES)
            out_ref[size * i : size * (i + 1), :] = x_ref[:, pl.ds(at, LANES)]
        base = size * (half // LANES)
        for i in range(inv_ref.shape[1] // LANES):
            at = pl.multiple_of(which * rows, rows)
            high, low = split(inv_ref[pl.ds(at, rows), LANES * i : LANES * (i + 1)])
            out_ref[base + rows * i : base + rows * (i + 1), :] = high
            shift = base + rows * (inv_ref.shape[1] // LANES)
            out_ref[shift + rows * i : shift + rows * (i + 1), :] = low


def prep(at, centres_cols, diag_inverse, quarter):
    size, width = centres_cols.shape
    total = (quarter * width // CORES + 2 * quarter // CORES * size) // LANES
    out = jax.ShapeDtypeStruct((total, LANES), jnp.bfloat16)
    whole = pl.BlockSpec((total, LANES), lambda i, at: (0, 0))
    return pl.pallas_call(
        prep_body,
        grid_spec=pltpu.PrefetchScalarGridSpec(
            num_scalar_prefetch=1,
            grid=(1,),
            in_specs=[
                pl.BlockSpec((quarter, width), lambda i, at: (at[0], 0)),
                pl.BlockSpec((quarter, size), lambda i, at: (at[0], 0)),
            ],
            out_specs=[whole, whole],
        ),
        out_shape=[out, out],
        name="prep",
    )(at, centres_cols, diag_inverse)


def update_body(at_ref, cols_ref, rows_ref, mine_ref, other_ref, trailing_ref, out_ref,
                x_ref, high_ref, low_ref, left_ref, left_low_ref, right_ref, right_low_ref):
    size, width = cols_ref.shape
    half = width // CORES
    quarters = mine_ref.shape[0]
    quarter = size // quarters
    part = quarter // CORES
    groups, inv_groups = half // LANES, size // LANES
    core = at_ref[1]
    for k, (got, which) in enumerate(((mine_ref, core), (other_ref, 1 - core))):
        for q in range(quarters):
            for i in range(groups):
                at = pl.multiple_of(which * half + LANES * i, LANES)
                x_ref[quarter * q : quarter * (q + 1), pl.ds(at, LANES)] = got[q, quarter * i : quarter * (i + 1), :]
            to = (k * quarters + q) * part
            for n, inv_ref in enumerate((high_ref, low_ref)):
                for i in range(inv_groups):
                    base = quarter * groups + (n * inv_groups + i) * part
                    inv_ref[to : to + part, LANES * i : LANES * (i + 1)] = got[q, base : base + part, :]

    x = x_ref[...]
    wide = x.astype(jnp.float32)
    ones = jnp.ones((8, width), jnp.bfloat16)
    square, square_low = split(wide * wide)
    sums = dot_t(ones, square) + dot_t(ones, square_low)
    norm_x = jnp.sqrt(sums[:1] + 1e-06)
    inv_x = 1.0 / norm_x

    for from_ref, to_ref, to_low_ref in ((cols_ref, right_ref, right_low_ref), (rows_ref, left_ref, left_low_ref)):
        for s in range(0, size, STEP):
            block = from_ref[s : s + STEP, :]
            gram = dot_t(block, x_ref[...])
            block = block.astype(jnp.float32)
            norm = jnp.sqrt(jnp.sum(block * block, axis=1, keepdims=True) + 1e-06)
            cosine = jnp.clip(gram * (1.0 / norm) * inv_x, -1.0, 1.0)
            values, values_low = split(layers(cosine) * (norm * norm_x))
            solved = dot_t(values, high_ref[...]) + (dot_t(values, low_ref[...]) + dot_t(values_low, high_ref[...]))
            solved, solved_low = split(solved)
            to_ref[s : s + STEP, :] = solved
            to_low_ref[s : s + STEP, :] = solved_low

    later = at_ref[2] > 0
    for s in range(0, size, STEP):
        left, left_low = left_ref[s : s + STEP, :], left_low_ref[s : s + STEP, :]
        update = dot_t(left, right_ref[...]) + (dot_t(left, right_low_ref[...]) + dot_t(left_low, right_ref[...]))
        old = trailing_ref[s : s + STEP, :]
        out_ref[s : s + STEP, :] = jnp.where(later, old - update, old)


def update(at, cols, rows, mine, other, trailing):
    size, width = cols.shape
    square = pltpu.VMEM((size, size), jnp.bfloat16)
    vmem = pl.BlockSpec(memory_space=pltpu.VMEM)
    return pl.pallas_call(
        update_body,
        in_specs=[pl.BlockSpec(memory_space=pltpu.SMEM)] + [vmem] * 5,
        out_specs=vmem,
        out_shape=jax.ShapeDtypeStruct(trailing.shape, trailing.dtype),
        scratch_shapes=[pltpu.VMEM((size, width), jnp.bfloat16)] + [square] * 6,
        compiler_params=pltpu.CompilerParams(vmem_limit_bytes=32 * 2**20),
        name="update",
    )(at, cols, rows, mine, other, trailing)


def on_device(chips, row_count, panel, centres_cols, centres_rows, diag_inverse, trailing):
    size, width = centres_cols.shape
    blocks = panel.shape[0]
    target_rank = blocks // 4
    quarter = size // row_count
    panel_at = jnp.sum(jnp.where(panel == target_rank, jnp.arange(blocks, dtype=jnp.int32), 0))
    owner_chip, owner_core = panel_at // CORES, panel_at % CORES
    chip, core, row = lax.axis_index("chip"), lax.axis_index("core"), lax.axis_index("row")
    own_rank = lax.dynamic_index_in_dim(panel, chip * CORES + core, 0, keepdims=False)
    at = jnp.stack([row, core, (own_rank > target_rank).astype(jnp.int32)]).astype(jnp.int32)
    swap = [(0, 1), (1, 0)]

    rows = lax.all_gather(centres_rows, ("chip", "core"), axis=0, tiled=True)

    kept, sent = prep(at, centres_cols, diag_inverse, quarter)
    taken = jnp.where(core == owner_core, kept, lax.ppermute(sent, "core", swap))
    per_chip = taken.shape[0] // chips
    incoming = lax.all_to_all(taken.reshape(chips, per_chip, LANES), "chip", 0, 0)
    piece = lax.dynamic_index_in_dim(incoming, owner_chip, 0, keepdims=False)

    mine = repeat_gather(piece, "chip", chips).reshape(taken.shape)
    all_mine = repeat_gather(mine, "row", row_count)
    all_other = lax.ppermute(all_mine, "core", swap)
    return update(at, centres_cols, rows, all_mine, all_other, trailing)


def solution(mesh):
    col_count, row_count = mesh.devices.shape
    chips = col_count // CORES
    fine = Mesh(mesh.devices.reshape(chips, CORES, row_count), ("chip", "core", "row"))

    def step(*arrays):
        return on_device(chips, row_count, *arrays)

    col = ("chip", "core")
    return jax.shard_map(
        step,
        mesh=fine,
        in_specs=(P(), P(col, None), P(("row",) + col, None), P(col, None), P("row", col)),
        out_specs=P("row", col),
        check_vma=False,
    )
```

```python
import math

import jax
import jax.numpy as jnp
from jax import lax
from jax.experimental import pallas as pl
from jax.experimental.pallas import tpu as pltpu
from jax.sharding import Mesh, PartitionSpec as P

LAYERS = 3
CORES = 2
LANES = 128
STEP = 64
WIDE = (0.4999999720071538, -0.06830646500676399, 0.028277340639243406, -0.01566003030791659,
        0.008837209300279753, -0.003820798788545866, 0.0008313362870811599)
NARROW = (0.4999769000530011, -0.06803611787881512, 0.026989768593852003, -0.012483028758839653,
          0.004564983607401579, -0.0008544733222650566)


def repeat_gather(piece, axis, count):
    return lax.all_to_all(jnp.broadcast_to(piece[None], (count,) + piece.shape), axis, 0, 0)


def split(values):
    high = values.astype(jnp.bfloat16)
    return high, (values - high.astype(jnp.float32)).astype(jnp.bfloat16)


def dot_t(left, right):
    return lax.dot_general(left, right, (((1,), (1,)), ((), ())), preferred_element_type=jnp.float32)


def poly(x, coefs):
    total = coefs[-1]
    for coef in coefs[-2::-1]:
        total = total * x + coef
    return total


def layers(rho):
    theta = rho
    for layer in range(LAYERS):
        size = jnp.abs(rho) if layer == 0 else rho
        rest = jnp.maximum(1.0 - size, 1e-30)
        below = rest * lax.rsqrt(rest)
        above = 1.0 + size
        above = above * lax.rsqrt(above) * (1.0 / math.pi)
        angle = below * poly(size, NARROW if layer == 2 else WIDE)
        zero_order = 1.0 - angle
        if layer == 0:
            zero_order = jnp.where(rho < 0.0, angle, zero_order)
        rho_next = below * above + zero_order * rho
        theta = theta * zero_order + rho_next
        rho = rho_next
    return theta


def prep_body(x_hbm, inv_hbm, rows_ref, kept_ref, sent_ref, x_ref, inv_ref, sems):
    row, core = lax.axis_index("row"), lax.axis_index("core")
    size, width = x_ref.shape
    take = pl.ds(pl.multiple_of(row * size, size), size)
    copy_x = pltpu.make_async_copy(x_hbm.at[take, :], x_ref, sems.at[0])
    copy_inv = pltpu.make_async_copy(inv_hbm.at[take, :], inv_ref, sems.at[1])
    copy_x.start()
    copy_inv.start()
    half, groups = width // CORES, inv_ref.shape[1] // LANES
    rows = size // CORES
    base = size * (half // LANES)
    end = base + 2 * rows * groups
    count = rows_ref.shape[0]
    for out_ref in (kept_ref, sent_ref):
        out_ref[end:, :] = jnp.zeros((kept_ref.shape[0] - end, LANES), jnp.bfloat16)
        for which in range(CORES):

            @pl.when(core == which)
            def _():
                for i in range(width // LANES):
                    to = end + CORES * count * i + count * which
                    out_ref[to : to + count, :] = rows_ref[:, LANES * i : LANES * (i + 1)]

    copy_x.wait()
    for out_ref, which in ((kept_ref, core), (sent_ref, 1 - core)):
        for i in range(half // LANES):
            at = pl.multiple_of(which * half + LANES * i, LANES)
            out_ref[size * i : size * (i + 1), :] = x_ref[:, pl.ds(at, LANES)]
    copy_inv.wait()
    for out_ref, which in ((kept_ref, core), (sent_ref, 1 - core)):
        for i in range(groups):
            at = pl.multiple_of(which * rows, rows)
            high, low = split(inv_ref[pl.ds(at, rows), LANES * i : LANES * (i + 1)])
            out_ref[base + rows * i : base + rows * (i + 1), :] = high
            shift = base + rows * groups
            out_ref[shift + rows * i : shift + rows * (i + 1), :] = low


VMEM = pl.BlockSpec(memory_space=pltpu.VMEM)
SMEM = pl.BlockSpec(memory_space=pltpu.SMEM)
ANY = pl.BlockSpec(memory_space=pl.ANY)


def prep(centres_cols, diag_inverse, centres_rows, quarter):
    size, width = centres_cols.shape
    total = (quarter * width // CORES + 2 * quarter // CORES * size + CORES * centres_rows.size) // LANES
    out = jax.ShapeDtypeStruct((total, LANES), jnp.bfloat16)
    return pl.pallas_call(
        prep_body,
        in_specs=[ANY, ANY, VMEM],
        out_specs=[VMEM, VMEM],
        out_shape=[out, out],
        scratch_shapes=[
            pltpu.VMEM((quarter, width), jnp.bfloat16),
            pltpu.VMEM((quarter, size), jnp.float32),
            pltpu.SemaphoreType.DMA((2,)),
        ],
        name="prep",
    )(centres_cols, diag_inverse, centres_rows)


def first_body(at_ref, kept_ref, got_ref, out_ref, later_ref):
    chips, length, _ = out_ref.shape
    per_chip = length // 2
    total = chips * per_chip
    kept = at_ref[3] > 0
    out_ref[:, :per_chip, :] = jnp.where(kept, kept_ref[:total], got_ref[:total]).reshape(chips, per_chip, LANES)
    for n in range(2):
        at = pl.ds(pl.multiple_of(total + (2 * at_ref[1] + n) * per_chip, per_chip), per_chip)
        rows = (kept_ref[at, :].astype(jnp.float32) + got_ref[at, :].astype(jnp.float32)).astype(jnp.bfloat16)
        if n == 0:
            out_ref[:, per_chip:, :] = jnp.broadcast_to(rows[None], (chips, per_chip, LANES))
        else:
            later_ref[...] = rows


def first_operand(at, kept, got, chips, per_chip):
    return pl.pallas_call(
        first_body,
        in_specs=[SMEM, VMEM, VMEM],
        out_specs=[VMEM, VMEM],
        out_shape=[
            jax.ShapeDtypeStruct((chips, 2 * per_chip, LANES), jnp.bfloat16),
            jax.ShapeDtypeStruct((per_chip, LANES), jnp.bfloat16),
        ],
        name="first_operand",
    )(at, kept, got)


def second_body(at_ref, came_ref, rows_ref, out_ref):
    chips, length, _ = out_ref.shape
    per_chip = length // 2
    piece = came_ref[at_ref[4], :per_chip, :]
    out_ref[:, :per_chip, :] = jnp.broadcast_to(piece[None], (chips, per_chip, LANES))
    out_ref[:, per_chip:, :] = jnp.broadcast_to(rows_ref[...][None], (chips, per_chip, LANES))


def second_operand(at, came, rows):
    return pl.pallas_call(
        second_body,
        in_specs=[SMEM, VMEM, VMEM],
        out_specs=VMEM,
        out_shape=jax.ShapeDtypeStruct(came.shape, came.dtype),
        name="second_operand",
    )(at, came, rows)


def third_body(came_ref, out_ref):
    per_chip = came_ref.shape[1] // 2
    piece = came_ref[:, :per_chip, :].reshape(out_ref.shape[1:])
    for q in range(out_ref.shape[0]):
        out_ref[q] = piece


def third_operand(came, row_count):
    chips, length, _ = came.shape
    return pl.pallas_call(
        third_body,
        in_specs=[VMEM],
        out_specs=VMEM,
        out_shape=jax.ShapeDtypeStruct((row_count, chips * length // 2, LANES), came.dtype),
        name="third_operand",
    )(came)


def update_body(at_ref, cols_ref, col_norm_ref, rows_own_ref, rows_other_ref, row_norm_ref, mine_ref, other_ref, trailing_ref, out_ref,
                x_ref, high_ref, low_ref, left_ref, left_low_ref, right_ref, right_low_ref,
                rows_ref, k_ref, k_low_ref, gram_ref, norm_ref, inv_ref):
    size, width = cols_ref.shape
    half = width // CORES
    quarters = mine_ref.shape[0]
    quarter = size // quarters
    part = quarter // CORES
    groups, inv_groups = half // LANES, size // LANES
    core = at_ref[1]
    for k, (got, which) in enumerate(((mine_ref, core), (other_ref, 1 - core))):
        for q in range(quarters):
            for i in range(groups):
                at = pl.multiple_of(which * half + LANES * i, LANES)
                x_ref[quarter * q : quarter * (q + 1), pl.ds(at, LANES)] = got[q, quarter * i : quarter * (i + 1), :]
            to = (k * quarters + q) * part
            for n, part_ref in enumerate((high_ref, low_ref)):
                for i in range(inv_groups):
                    base = quarter * groups + (n * inv_groups + i) * part
                    part_ref[to : to + part, LANES * i : LANES * (i + 1)] = got[q, base : base + part, :]

    for got, which in ((rows_own_ref, core), (rows_other_ref, 1 - core)):
        rows_ref[:, pl.ds(pl.multiple_of(which * half, half), half)] = got[...]

    wide = x_ref[...].astype(jnp.float32)
    norm_x = jnp.sqrt(jnp.sum(wide * wide, axis=1, keepdims=True) + 1e-06)
    norm_x = jnp.broadcast_to(norm_x, (size, LANES)).T[:STEP]
    norm_ref[...] = norm_x
    inv_ref[...] = 1.0 / norm_x

    for from_ref, from_norm_ref, to_ref, to_low_ref in (
        (cols_ref, col_norm_ref, right_ref, right_low_ref),
        (rows_ref, row_norm_ref, left_ref, left_low_ref),
    ):
        gram_ref[...] = dot_t(from_ref[...], x_ref[...])

        @pl.loop(0, size // STEP)
        def _(i):
            at = pl.ds(pl.multiple_of(i * STEP, STEP), STEP)
            norm = jnp.concatenate([from_norm_ref[at, :]] * (size // LANES), axis=1)
            cosine = gram_ref[at, :] * (1.0 / norm) * inv_ref[...]
            values = layers(jnp.clip(cosine, -1.0, 1.0)) * (norm * norm_ref[...])
            values, values_low = split(values)
            k_ref[at, :] = values
            k_low_ref[at, :] = values_low

        solved = dot_t(k_ref[...], high_ref[...]) + (dot_t(k_ref[...], low_ref[...]) + dot_t(k_low_ref[...], high_ref[...]))
        solved, solved_low = split(solved)
        to_ref[...] = solved
        to_low_ref[...] = solved_low

    update = dot_t(left_ref[...], right_ref[...]) + (dot_t(left_ref[...], right_low_ref[...]) + dot_t(left_low_ref[...], right_ref[...]))
    old = trailing_ref[...]
    out_ref[...] = jnp.where(at_ref[2] > 0, old - update, old)


def norms(*pieces):
    total = 1e-06
    for piece in pieces:
        wide = piece.astype(jnp.float32)
        total += jnp.sum(wide * wide, axis=1, keepdims=True)
    return jnp.broadcast_to(jnp.sqrt(total), (pieces[0].shape[0], LANES))


def update(at, cols, rows_own, rows_other, mine, other, trailing):
    size, width = cols.shape
    square = pltpu.VMEM((size, size), jnp.bfloat16)
    vectors = pltpu.VMEM((size, width), jnp.bfloat16)
    return pl.pallas_call(
        update_body,
        in_specs=[SMEM] + [VMEM] * 8,
        out_specs=VMEM,
        out_shape=jax.ShapeDtypeStruct(trailing.shape, trailing.dtype),
        scratch_shapes=[vectors]
        + [square] * 6
        + [vectors]
        + [square] * 2
        + [pltpu.VMEM((size, size), jnp.float32)]
        + [pltpu.VMEM((STEP, size), jnp.float32)] * 2,
        compiler_params=pltpu.CompilerParams(vmem_limit_bytes=32 * 2**20),
        name="update",
    )(at, cols, norms(cols), rows_own, rows_other, norms(rows_own, rows_other), mine, other, trailing)


def on_device(chips, row_count, panel, centres_cols, centres_rows, diag_inverse, trailing):
    size, width = centres_cols.shape
    blocks = panel.shape[0]
    target_rank = blocks // 4
    quarter = size // row_count
    panel_at = jnp.sum(jnp.where(panel == target_rank, jnp.arange(blocks, dtype=jnp.int32), 0))
    owner_chip, owner_core = panel_at // CORES, panel_at % CORES
    chip, core, row = lax.axis_index("chip"), lax.axis_index("core"), lax.axis_index("row")
    own_rank = lax.dynamic_index_in_dim(panel, chip * CORES + core, 0, keepdims=False)
    flags = [row, core, own_rank > target_rank, core == owner_core, owner_chip]
    at = jnp.stack([flag.astype(jnp.int32) for flag in flags])
    swap = [(0, 1), (1, 0)]

    kept, sent = prep(centres_cols, diag_inverse, centres_rows, quarter)
    got = lax.ppermute(sent, "core", swap)
    per_chip = (2 * width * quarter // CORES) // (LANES * chips)
    outgoing, rows_later = first_operand(at, kept, got, chips, per_chip)
    first = lax.all_to_all(outgoing, "chip", 0, 0)
    second = lax.all_to_all(second_operand(at, first, rows_later), "chip", 0, 0)
    all_mine = lax.all_to_all(third_operand(second, row_count), "row", 0, 0)

    tiles = [got_rows[:, i : i + 8] for got_rows in (first, second) for i in range(per_chip, 2 * per_chip, 8)]
    rows_own = jnp.concatenate([tile.reshape(size, LANES) for tile in tiles], axis=1)
    rows_other = lax.ppermute(rows_own, "core", swap)
    all_other = lax.ppermute(all_mine, "core", swap)
    return update(at, centres_cols, rows_own, rows_other, all_mine, all_other, trailing)


def solution(mesh):
    col_count, row_count = mesh.devices.shape
    chips = col_count // CORES
    fine = Mesh(mesh.devices.reshape(chips, CORES, row_count), ("chip", "core", "row"))

    def step(*arrays):
        return on_device(chips, row_count, *arrays)

    col = ("chip", "core")
    return jax.shard_map(
        step,
        mesh=fine,
        in_specs=(P(), P(col, None), P(("row",) + col, None), P(col, None), P("row", col)),
        out_specs=P("row", col),
        check_vma=False,
    )
```

```python
import math

import jax
import jax.numpy as jnp
from jax import lax
from jax.experimental import pallas as pl
from jax.experimental.pallas import tpu as pltpu
from jax.sharding import Mesh, PartitionSpec as P

LAYERS = 3
CORES = 2
LANES = 128
STEP = 64
WIDE = (0.4999999720071538, -0.06830646500676399, 0.028277340639243406, -0.01566003030791659,
        0.008837209300279753, -0.003820798788545866, 0.0008313362870811599)
NARROW = (0.4999769000530011, -0.06803611787881512, 0.026989768593852003, -0.012483028758839653,
          0.004564983607401579, -0.0008544733222650566)


def repeat_gather(piece, axis, count):
    return lax.all_to_all(jnp.broadcast_to(piece[None], (count,) + piece.shape), axis, 0, 0)


def split(values):
    high = values.astype(jnp.bfloat16)
    return high, (values - high.astype(jnp.float32)).astype(jnp.bfloat16)


def dot_t(left, right):
    return lax.dot_general(left, right, (((1,), (1,)), ((), ())), preferred_element_type=jnp.float32)


def poly(x, coefs):
    total = coefs[-1]
    for coef in coefs[-2::-1]:
        total = total * x + coef
    return total


def layers(rho):
    theta = rho
    for layer in range(LAYERS):
        size = jnp.abs(rho) if layer == 0 else rho
        rest = jnp.maximum(1.0 - size, 1e-30)
        below = rest * lax.rsqrt(rest)
        above = 1.0 + size
        above = above * lax.rsqrt(above) * (1.0 / math.pi)
        angle = below * poly(size, NARROW if layer == 2 else WIDE)
        zero_order = 1.0 - angle
        if layer == 0:
            zero_order = jnp.where(rho < 0.0, angle, zero_order)
        rho_next = below * above + zero_order * rho
        theta = theta * zero_order + rho_next
        rho = rho_next
    return theta


def prep_body(x_hbm, inv_hbm, rows_ref, kept_ref, sent_ref, x_ref, inv_ref, sems):
    row, core = lax.axis_index("row"), lax.axis_index("core")
    size, width = x_ref.shape
    take = pl.ds(pl.multiple_of(row * size, size), size)
    copy_x = pltpu.make_async_copy(x_hbm.at[take, :], x_ref, sems.at[0])
    copy_inv = pltpu.make_async_copy(inv_hbm.at[take, :], inv_ref, sems.at[1])
    copy_x.start()
    copy_inv.start()
    half, groups = width // CORES, inv_ref.shape[1] // LANES
    rows = size // CORES
    base = size * (half // LANES)
    end = base + 2 * rows * groups
    count = rows_ref.shape[0]
    for out_ref in (kept_ref, sent_ref):
        out_ref[end:, :] = jnp.zeros((kept_ref.shape[0] - end, LANES), jnp.bfloat16)
        for which in range(CORES):

            @pl.when(core == which)
            def _():
                for i in range(width // LANES):
                    to = end + CORES * count * i + count * which
                    out_ref[to : to + count, :] = rows_ref[:, LANES * i : LANES * (i + 1)]

    copy_x.wait()
    for out_ref, which in ((kept_ref, core), (sent_ref, 1 - core)):
        for i in range(half // LANES):
            at = pl.multiple_of(which * half + LANES * i, LANES)
            out_ref[size * i : size * (i + 1), :] = x_ref[:, pl.ds(at, LANES)]
    copy_inv.wait()
    for out_ref, which in ((kept_ref, core), (sent_ref, 1 - core)):
        for i in range(groups):
            at = pl.multiple_of(which * rows, rows)
            high, low = split(inv_ref[pl.ds(at, rows), LANES * i : LANES * (i + 1)])
            out_ref[base + rows * i : base + rows * (i + 1), :] = high
            shift = base + rows * groups
            out_ref[shift + rows * i : shift + rows * (i + 1), :] = low


VMEM = pl.BlockSpec(memory_space=pltpu.VMEM)
SMEM = pl.BlockSpec(memory_space=pltpu.SMEM)
HBM = pl.BlockSpec(memory_space=pltpu.HBM)
SMALL = pltpu.CompilerParams(vmem_limit_bytes=4 * 2**20)


def prep(centres_cols, diag_inverse, centres_rows, quarter):
    size, width = centres_cols.shape
    total = (quarter * width // CORES + 2 * quarter // CORES * size + CORES * centres_rows.size) // LANES
    out = jax.ShapeDtypeStruct((total, LANES), jnp.bfloat16)
    return pl.pallas_call(
        prep_body,
        in_specs=[HBM, HBM, VMEM],
        out_specs=[VMEM, VMEM],
        out_shape=[out, out],
        scratch_shapes=[
            pltpu.VMEM((quarter, width), jnp.bfloat16),
            pltpu.VMEM((quarter, size), jnp.float32),
            pltpu.SemaphoreType.DMA((2,)),
        ],
        compiler_params=SMALL,
        name="prep",
    )(centres_cols, diag_inverse, centres_rows)


def first_body(at_ref, kept_ref, got_ref, out_ref, later_ref):
    chips, length, _ = out_ref.shape
    per_chip = length // 2
    total = chips * per_chip
    kept = at_ref[3] > 0
    out_ref[:, :per_chip, :] = jnp.where(kept, kept_ref[:total], got_ref[:total]).reshape(chips, per_chip, LANES)
    for n in range(2):
        at = pl.ds(pl.multiple_of(total + (2 * at_ref[1] + n) * per_chip, per_chip), per_chip)
        rows = (kept_ref[at, :].astype(jnp.float32) + got_ref[at, :].astype(jnp.float32)).astype(jnp.bfloat16)
        if n == 0:
            out_ref[:, per_chip:, :] = jnp.broadcast_to(rows[None], (chips, per_chip, LANES))
        else:
            later_ref[...] = rows


def first_operand(at, kept, got, chips, per_chip):
    return pl.pallas_call(
        first_body,
        in_specs=[SMEM, VMEM, VMEM],
        out_specs=[VMEM, VMEM],
        out_shape=[
            jax.ShapeDtypeStruct((chips, 2 * per_chip, LANES), jnp.bfloat16),
            jax.ShapeDtypeStruct((per_chip, LANES), jnp.bfloat16),
        ],
        compiler_params=SMALL,
        name="first_operand",
    )(at, kept, got)


def second_body(at_ref, came_ref, rows_ref, out_ref):
    chips, length, _ = out_ref.shape
    per_chip = length // 2
    piece = came_ref[at_ref[4], :per_chip, :]
    out_ref[:, :per_chip, :] = jnp.broadcast_to(piece[None], (chips, per_chip, LANES))
    out_ref[:, per_chip:, :] = jnp.broadcast_to(rows_ref[...][None], (chips, per_chip, LANES))


def second_operand(at, came, rows):
    return pl.pallas_call(
        second_body,
        in_specs=[SMEM, VMEM, VMEM],
        out_specs=VMEM,
        out_shape=jax.ShapeDtypeStruct(came.shape, came.dtype),
        compiler_params=SMALL,
        name="second_operand",
    )(at, came, rows)


def third_body(came_ref, out_ref):
    per_chip = came_ref.shape[1] // 2
    piece = came_ref[:, :per_chip, :].reshape(out_ref.shape[1:])
    for q in range(out_ref.shape[0]):
        out_ref[q] = piece


def third_operand(came, row_count):
    chips, length, _ = came.shape
    return pl.pallas_call(
        third_body,
        in_specs=[VMEM],
        out_specs=VMEM,
        out_shape=jax.ShapeDtypeStruct((row_count, chips * length // 2, LANES), came.dtype),
        compiler_params=SMALL,
        name="third_operand",
    )(came)


def update_body(at_ref, cols_ref, col_norm_ref, rows_own_ref, rows_other_ref, row_norm_ref, mine_ref, other_ref, trailing_ref, out_ref,
                x_ref, high_ref, low_ref, left_ref, left_low_ref, right_ref, right_low_ref,
                rows_ref, k_ref, k_low_ref, gram_ref, norm_ref, inv_ref):
    size, width = cols_ref.shape
    half = width // CORES
    quarters = mine_ref.shape[0]
    quarter = size // quarters
    part = quarter // CORES
    groups, inv_groups = half // LANES, size // LANES
    core = at_ref[1]
    for k, (got, which) in enumerate(((mine_ref, core), (other_ref, 1 - core))):
        for q in range(quarters):
            for i in range(groups):
                at = pl.multiple_of(which * half + LANES * i, LANES)
                x_ref[quarter * q : quarter * (q + 1), pl.ds(at, LANES)] = got[q, quarter * i : quarter * (i + 1), :]
            to = (k * quarters + q) * part
            for n, part_ref in enumerate((high_ref, low_ref)):
                for i in range(inv_groups):
                    base = quarter * groups + (n * inv_groups + i) * part
                    part_ref[to : to + part, LANES * i : LANES * (i + 1)] = got[q, base : base + part, :]

    for got, which in ((rows_own_ref, core), (rows_other_ref, 1 - core)):
        rows_ref[:, pl.ds(pl.multiple_of(which * half, half), half)] = got[...]

    wide = x_ref[...].astype(jnp.float32)
    norm_x = jnp.sqrt(jnp.sum(wide * wide, axis=1, keepdims=True) + 1e-06)
    norm_x = jnp.broadcast_to(norm_x, (size, LANES)).T[:STEP]
    norm_ref[...] = norm_x
    inv_ref[...] = 1.0 / norm_x

    for from_ref, from_norm_ref, to_ref, to_low_ref in (
        (cols_ref, col_norm_ref, right_ref, right_low_ref),
        (rows_ref, row_norm_ref, left_ref, left_low_ref),
    ):
        gram_ref[...] = dot_t(from_ref[...], x_ref[...])

        @pl.loop(0, size // STEP)
        def _(i):
            at = pl.ds(pl.multiple_of(i * STEP, STEP), STEP)
            norm = jnp.concatenate([from_norm_ref[at, :]] * (size // LANES), axis=1)
            cosine = gram_ref[at, :] * (1.0 / norm) * inv_ref[...]
            values = layers(jnp.clip(cosine, -1.0, 1.0)) * (norm * norm_ref[...])
            values, values_low = split(values)
            k_ref[at, :] = values
            k_low_ref[at, :] = values_low

        solved = dot_t(k_ref[...], high_ref[...]) + (dot_t(k_ref[...], low_ref[...]) + dot_t(k_low_ref[...], high_ref[...]))
        solved, solved_low = split(solved)
        to_ref[...] = solved
        to_low_ref[...] = solved_low

    update = dot_t(left_ref[...], right_ref[...]) + (dot_t(left_ref[...], right_low_ref[...]) + dot_t(left_low_ref[...], right_ref[...]))
    old = trailing_ref[...]
    out_ref[...] = jnp.where(at_ref[2] > 0, old - update, old)


def norms(*pieces):
    total = 1e-06
    for piece in pieces:
        wide = piece.astype(jnp.float32)
        total += jnp.sum(wide * wide, axis=1, keepdims=True)
    return jnp.broadcast_to(jnp.sqrt(total), (pieces[0].shape[0], LANES))


def update(at, cols, rows_own, rows_other, mine, other, trailing):
    size, width = cols.shape
    square = pltpu.VMEM((size, size), jnp.bfloat16)
    vectors = pltpu.VMEM((size, width), jnp.bfloat16)
    return pl.pallas_call(
        update_body,
        in_specs=[SMEM] + [VMEM] * 8,
        out_specs=VMEM,
        out_shape=jax.ShapeDtypeStruct(trailing.shape, trailing.dtype),
        scratch_shapes=[vectors]
        + [square] * 6
        + [vectors]
        + [square] * 2
        + [pltpu.VMEM((size, size), jnp.float32)]
        + [pltpu.VMEM((STEP, size), jnp.float32)] * 2,
        compiler_params=pltpu.CompilerParams(vmem_limit_bytes=20 * 2**20),
        name="update",
    )(at, cols, norms(cols), rows_own, rows_other, norms(rows_own, rows_other), mine, other, trailing)


def on_device(chips, row_count, panel, centres_cols, centres_rows, diag_inverse, trailing):
    size, width = centres_cols.shape
    blocks = panel.shape[0]
    target_rank = blocks // 4
    quarter = size // row_count
    panel_at = jnp.sum(jnp.where(panel == target_rank, jnp.arange(blocks, dtype=jnp.int32), 0))
    owner_chip, owner_core = panel_at // CORES, panel_at % CORES
    chip, core, row = lax.axis_index("chip"), lax.axis_index("core"), lax.axis_index("row")
    own_rank = lax.dynamic_index_in_dim(panel, chip * CORES + core, 0, keepdims=False)
    flags = [row, core, own_rank > target_rank, core == owner_core, owner_chip]
    at = jnp.stack([flag.astype(jnp.int32) for flag in flags])
    swap = [(0, 1), (1, 0)]

    kept, sent = prep(centres_cols, diag_inverse, centres_rows, quarter)
    got = lax.ppermute(sent, "core", swap)
    per_chip = (2 * width * quarter // CORES) // (LANES * chips)
    outgoing, rows_later = first_operand(at, kept, got, chips, per_chip)
    first = lax.all_to_all(outgoing, "chip", 0, 0)
    second = lax.all_to_all(second_operand(at, first, rows_later), "chip", 0, 0)
    all_mine = lax.all_to_all(third_operand(second, row_count), "row", 0, 0)

    tiles = [got_rows[:, i : i + 8] for got_rows in (first, second) for i in range(per_chip, 2 * per_chip, 8)]
    rows_own = jnp.concatenate([tile.reshape(size, LANES) for tile in tiles], axis=1)
    rows_other = lax.ppermute(rows_own, "core", swap)
    all_other = lax.ppermute(all_mine, "core", swap)
    return update(at, centres_cols, rows_own, rows_other, all_mine, all_other, trailing)


def solution(mesh):
    col_count, row_count = mesh.devices.shape
    chips = col_count // CORES
    fine = Mesh(mesh.devices.reshape(chips, CORES, row_count), ("chip", "core", "row"))

    def step(*arrays):
        return on_device(chips, row_count, *arrays)

    col = ("chip", "core")
    return jax.shard_map(
        step,
        mesh=fine,
        in_specs=(P(), P(col, None), P(("row",) + col, None), P(col, None), P("row", col)),
        out_specs=P("row", col),
        check_vma=False,
    )
```

```python
import math

import jax
import jax.numpy as jnp
from jax import lax
from jax.experimental import pallas as pl
from jax.experimental.pallas import tpu as pltpu
from jax.sharding import Mesh, PartitionSpec as P

LAYERS = 3
CORES = 2
LANES = 128
STEP = 64
WIDE = (0.4999999720071538, -0.06830646500676399, 0.028277340639243406, -0.01566003030791659,
        0.008837209300279753, -0.003820798788545866, 0.0008313362870811599)
NARROW = (0.4999769000530011, -0.06803611787881512, 0.026989768593852003, -0.012483028758839653,
          0.004564983607401579, -0.0008544733222650566)


def repeat_gather(piece, axis, count):
    return lax.all_to_all(jnp.broadcast_to(piece[None], (count,) + piece.shape), axis, 0, 0)


def split(values):
    high = values.astype(jnp.bfloat16)
    return high, (values - high.astype(jnp.float32)).astype(jnp.bfloat16)


def dot_t(left, right):
    return lax.dot_general(left, right, (((1,), (1,)), ((), ())), preferred_element_type=jnp.float32)


def poly(x, coefs):
    total = coefs[-1]
    for coef in coefs[-2::-1]:
        total = total * x + coef
    return total


def layers(rho):
    theta = rho
    for layer in range(LAYERS):
        size = jnp.abs(rho) if layer == 0 else rho
        rest = jnp.maximum(1.0 - size, 1e-30)
        below = rest * lax.rsqrt(rest)
        above = 1.0 + size
        above = above * lax.rsqrt(above) * (1.0 / math.pi)
        angle = below * poly(size, NARROW if layer == 2 else WIDE)
        zero_order = 1.0 - angle
        if layer == 0:
            zero_order = jnp.where(rho < 0.0, angle, zero_order)
        rho_next = below * above + zero_order * rho
        theta = theta * zero_order + rho_next
        rho = rho_next
    return theta


def prep_body(x_ref, inv_ref, rows_ref, kept_ref, sent_ref):
    core = lax.axis_index("core")
    size, width = x_ref.shape
    half, groups = width // CORES, inv_ref.shape[1] // LANES
    rows = size // CORES
    base = size * (half // LANES)
    end = base + 2 * rows * groups
    count = rows_ref.shape[0]
    for out_ref in (kept_ref, sent_ref):
        out_ref[end:, :] = jnp.zeros((kept_ref.shape[0] - end, LANES), jnp.bfloat16)
        for which in range(CORES):

            @pl.when(core == which)
            def _():
                for i in range(width // LANES):
                    to = end + CORES * count * i + count * which
                    out_ref[to : to + count, :] = rows_ref[:, LANES * i : LANES * (i + 1)]

    for out_ref, which in ((kept_ref, core), (sent_ref, 1 - core)):
        for i in range(half // LANES):
            at = pl.multiple_of(which * half + LANES * i, LANES)
            out_ref[size * i : size * (i + 1), :] = x_ref[:, pl.ds(at, LANES)]
    for out_ref, which in ((kept_ref, core), (sent_ref, 1 - core)):
        for i in range(groups):
            at = pl.multiple_of(which * rows, rows)
            high, low = split(inv_ref[pl.ds(at, rows), LANES * i : LANES * (i + 1)])
            out_ref[base + rows * i : base + rows * (i + 1), :] = high
            shift = base + rows * groups
            out_ref[shift + rows * i : shift + rows * (i + 1), :] = low


VMEM = pl.BlockSpec(memory_space=pltpu.VMEM)
SMALL = pltpu.CompilerParams(vmem_limit_bytes=4 * 2**20)


def prep(x, inverse, rows):
    size, width = x.shape
    total = (width * size // CORES + 2 * inverse.size // CORES + CORES * rows.size) // LANES
    out = jax.ShapeDtypeStruct((total, LANES), jnp.bfloat16)
    return pl.pallas_call(
        prep_body,
        in_specs=[VMEM, VMEM, VMEM],
        out_specs=[VMEM, VMEM],
        out_shape=[out, out],
        compiler_params=SMALL,
        name="prep",
    )(x, inverse, rows)


def owner_of(panel_ref):
    blocks = panel_ref.shape[1]
    at = lax.broadcasted_iota(jnp.int32, (1, blocks), 1)
    found = jnp.where(panel_ref[...] == blocks // 4, at, 0).astype(jnp.float32)
    return jnp.sum(found).astype(jnp.int32)


def first_body(panel_ref, kept_ref, got_ref, out_ref, later_ref):
    chips, length, _ = out_ref.shape
    per_chip = length // 2
    total = chips * per_chip
    core = lax.axis_index("core")
    kept = owner_of(panel_ref) % CORES == core
    out_ref[:, :per_chip, :] = jnp.where(kept, kept_ref[:total], got_ref[:total]).reshape(chips, per_chip, LANES)
    for n in range(2):
        at = pl.ds(pl.multiple_of(total + (2 * core + n) * per_chip, per_chip), per_chip)
        rows = (kept_ref[at, :].astype(jnp.float32) + got_ref[at, :].astype(jnp.float32)).astype(jnp.bfloat16)
        if n == 0:
            out_ref[:, per_chip:, :] = jnp.broadcast_to(rows[None], (chips, per_chip, LANES))
        else:
            later_ref[...] = rows


def first_operand(panel, kept, got, chips, per_chip):
    return pl.pallas_call(
        first_body,
        in_specs=[VMEM, VMEM, VMEM],
        out_specs=[VMEM, VMEM],
        out_shape=[
            jax.ShapeDtypeStruct((chips, 2 * per_chip, LANES), jnp.bfloat16),
            jax.ShapeDtypeStruct((per_chip, LANES), jnp.bfloat16),
        ],
        compiler_params=SMALL,
        name="first_operand",
    )(panel, kept, got)


def second_body(panel_ref, came_ref, rows_ref, out_ref):
    chips, length, _ = out_ref.shape
    per_chip = length // 2
    piece = came_ref[owner_of(panel_ref) // CORES, :per_chip, :]
    out_ref[:, :per_chip, :] = jnp.broadcast_to(piece[None], (chips, per_chip, LANES))
    out_ref[:, per_chip:, :] = jnp.broadcast_to(rows_ref[...][None], (chips, per_chip, LANES))


def second_operand(panel, came, rows):
    return pl.pallas_call(
        second_body,
        in_specs=[VMEM, VMEM, VMEM],
        out_specs=VMEM,
        out_shape=jax.ShapeDtypeStruct(came.shape, came.dtype),
        compiler_params=SMALL,
        name="second_operand",
    )(panel, came, rows)


def third_body(came_ref, out_ref):
    per_chip = came_ref.shape[1] // 2
    piece = came_ref[:, :per_chip, :].reshape(out_ref.shape[1:])
    for q in range(out_ref.shape[0]):
        out_ref[q] = piece


def third_operand(came, row_count):
    chips, length, _ = came.shape
    return pl.pallas_call(
        third_body,
        in_specs=[VMEM],
        out_specs=VMEM,
        out_shape=jax.ShapeDtypeStruct((row_count, chips * length // 2, LANES), came.dtype),
        compiler_params=SMALL,
        name="third_operand",
    )(came)


def update_body(panel_ref, cols_ref, col_norm_ref, rows_own_ref, rows_other_ref, row_norm_ref, mine_ref, other_ref, trailing_ref, out_ref,
                x_ref, high_ref, low_ref, left_ref, left_low_ref, right_ref, right_low_ref,
                rows_ref, k_ref, k_low_ref, gram_ref, norm_ref, inv_ref):
    size, width = cols_ref.shape
    half = width // CORES
    quarters = mine_ref.shape[0]
    quarter = size // quarters
    part = quarter // CORES
    groups, inv_groups = half // LANES, size // LANES
    core = lax.axis_index("core")
    for k, (got, which) in enumerate(((mine_ref, core), (other_ref, 1 - core))):
        for q in range(quarters):
            for i in range(groups):
                at = pl.multiple_of(which * half + LANES * i, LANES)
                x_ref[quarter * q : quarter * (q + 1), pl.ds(at, LANES)] = got[q, quarter * i : quarter * (i + 1), :]
            to = (k * quarters + q) * part
            for n, part_ref in enumerate((high_ref, low_ref)):
                for i in range(inv_groups):
                    base = quarter * groups + (n * inv_groups + i) * part
                    part_ref[to : to + part, LANES * i : LANES * (i + 1)] = got[q, base : base + part, :]

    for got, which in ((rows_own_ref, core), (rows_other_ref, 1 - core)):
        rows_ref[:, pl.ds(pl.multiple_of(which * half, half), half)] = got[...]

    wide = x_ref[...].astype(jnp.float32)
    norm_x = jnp.sqrt(jnp.sum(wide * wide, axis=1, keepdims=True) + 1e-06)
    norm_x = jnp.broadcast_to(norm_x, (size, LANES)).T[:STEP]
    norm_ref[...] = norm_x
    inv_ref[...] = 1.0 / norm_x

    for from_ref, from_norm_ref, to_ref, to_low_ref in (
        (cols_ref, col_norm_ref, right_ref, right_low_ref),
        (rows_ref, row_norm_ref, left_ref, left_low_ref),
    ):
        gram_ref[...] = dot_t(from_ref[...], x_ref[...])

        @pl.loop(0, size // STEP)
        def _(i):
            at = pl.ds(pl.multiple_of(i * STEP, STEP), STEP)
            norm = jnp.concatenate([from_norm_ref[at, :]] * (size // LANES), axis=1)
            cosine = gram_ref[at, :] * (1.0 / norm) * inv_ref[...]
            values = layers(jnp.clip(cosine, -1.0, 1.0)) * (norm * norm_ref[...])
            values, values_low = split(values)
            k_ref[at, :] = values
            k_low_ref[at, :] = values_low

        solved = dot_t(k_ref[...], high_ref[...]) + (dot_t(k_ref[...], low_ref[...]) + dot_t(k_low_ref[...], high_ref[...]))
        solved, solved_low = split(solved)
        to_ref[...] = solved
        to_low_ref[...] = solved_low

    update = dot_t(left_ref[...], right_ref[...]) + (dot_t(left_ref[...], right_low_ref[...]) + dot_t(left_low_ref[...], right_ref[...]))
    blocks = panel_ref.shape[1]
    here = lax.broadcasted_iota(jnp.int32, (1, blocks), 1) == CORES * lax.axis_index("chip") + core
    own_rank = jnp.sum(jnp.where(here, panel_ref[...], 0).astype(jnp.float32))
    old = trailing_ref[...]
    out_ref[...] = jnp.where(own_rank > blocks // 4, old - update, old)


def norms(*pieces):
    total = 1e-06
    for piece in pieces:
        wide = piece.astype(jnp.float32)
        total += jnp.sum(wide * wide, axis=1, keepdims=True)
    return jnp.broadcast_to(jnp.sqrt(total), (pieces[0].shape[0], LANES))


def update(panel, cols, rows_own, rows_other, mine, other, trailing):
    size, width = cols.shape
    square = pltpu.VMEM((size, size), jnp.bfloat16)
    vectors = pltpu.VMEM((size, width), jnp.bfloat16)
    return pl.pallas_call(
        update_body,
        in_specs=[VMEM] * 9,
        out_specs=VMEM,
        out_shape=jax.ShapeDtypeStruct(trailing.shape, trailing.dtype),
        scratch_shapes=[vectors]
        + [square] * 6
        + [vectors]
        + [square] * 2
        + [pltpu.VMEM((size, size), jnp.float32)]
        + [pltpu.VMEM((STEP, size), jnp.float32)] * 2,
        compiler_params=pltpu.CompilerParams(vmem_limit_bytes=20 * 2**20),
        name="update",
    )(panel, cols, norms(cols), rows_own, rows_other, norms(rows_own, rows_other), mine, other, trailing)


def on_device(chips, row_count, panel, centres_cols, centres_rows, diag_inverse, trailing):
    size, width = centres_cols.shape
    quarter = size // row_count
    row = lax.axis_index("row")
    panel = panel[None]
    swap = [(0, 1), (1, 0)]

    x = lax.dynamic_slice_in_dim(centres_cols, row * quarter, quarter, 0)
    inverse = lax.dynamic_slice_in_dim(diag_inverse, row * quarter, quarter, 0)
    kept, sent = prep(x, inverse, centres_rows)
    got = lax.ppermute(sent, "core", swap)
    per_chip = (2 * width * quarter // CORES) // (LANES * chips)
    outgoing, rows_later = first_operand(panel, kept, got, chips, per_chip)
    first = lax.all_to_all(outgoing, "chip", 0, 0)
    second = lax.all_to_all(second_operand(panel, first, rows_later), "chip", 0, 0)
    all_mine = lax.all_to_all(third_operand(second, row_count), "row", 0, 0)

    tiles = [got_rows[:, i : i + 8] for got_rows in (first, second) for i in range(per_chip, 2 * per_chip, 8)]
    rows_own = jnp.concatenate([tile.reshape(size, LANES) for tile in tiles], axis=1)
    rows_other = lax.ppermute(rows_own, "core", swap)
    all_mine, rows_other = lax.optimization_barrier((all_mine, rows_other))
    all_other = lax.ppermute(all_mine, "core", swap)
    return update(panel, centres_cols, rows_own, rows_other, all_mine, all_other, trailing)


def solution(mesh):
    col_count, row_count = mesh.devices.shape
    chips = col_count // CORES
    fine = Mesh(mesh.devices.reshape(chips, CORES, row_count), ("chip", "core", "row"))

    def step(*arrays):
        return on_device(chips, row_count, *arrays)

    col = ("chip", "core")
    return jax.shard_map(
        step,
        mesh=fine,
        in_specs=(P(), P(col, None), P(("row",) + col, None), P(col, None), P("row", col)),
        out_specs=P("row", col),
        check_vma=False,
    )
```

```python
import math

import jax
import jax.numpy as jnp
from jax import lax
from jax.experimental import pallas as pl
from jax.experimental.pallas import tpu as pltpu
from jax.sharding import Mesh, PartitionSpec as P

LAYERS = 3
CORES = 2
LANES = 128
STEP = 128
WIDE = (0.4999999720071538, -0.06830646500676399, 0.028277340639243406, -0.01566003030791659,
        0.008837209300279753, -0.003820798788545866, 0.0008313362870811599)
NARROW = (0.4999769000530011, -0.06803611787881512, 0.026989768593852003, -0.012483028758839653,
          0.004564983607401579, -0.0008544733222650566)


def repeat_gather(piece, axis, count):
    return lax.all_to_all(jnp.broadcast_to(piece[None], (count,) + piece.shape), axis, 0, 0)


def split(values):
    high = values.astype(jnp.bfloat16)
    return high, (values - high.astype(jnp.float32)).astype(jnp.bfloat16)


def dot_t(left, right):
    return lax.dot_general(left, right, (((1,), (1,)), ((), ())), preferred_element_type=jnp.float32)


def poly(x, coefs):
    total = coefs[-1]
    for coef in coefs[-2::-1]:
        total = total * x + coef
    return total


def layers(rho):
    theta = rho
    for layer in range(LAYERS):
        size = jnp.abs(rho) if layer == 0 else rho
        rest = jnp.maximum(1.0 - size, 1e-30)
        below = rest * lax.rsqrt(rest)
        above = 1.0 + size
        above = above * lax.rsqrt(above) * (1.0 / math.pi)
        angle = below * poly(size, NARROW if layer == 2 else WIDE)
        zero_order = 1.0 - angle
        if layer == 0:
            zero_order = jnp.where(rho < 0.0, angle, zero_order)
        rho_next = below * above + zero_order * rho
        theta = theta * zero_order + rho_next
        rho = rho_next
    return theta


def prep_body(x_ref, inv_ref, rows_ref, kept_ref, sent_ref):
    core = lax.axis_index("core")
    _, part, width = x_ref.shape
    groups, inv_groups = width // LANES, inv_ref.shape[2] // LANES
    base = part * groups
    shift = base + part * inv_groups
    end = shift + part * inv_groups
    count = rows_ref.shape[0]
    for out_ref in (kept_ref, sent_ref):
        out_ref[end:, :] = jnp.zeros((kept_ref.shape[0] - end, LANES), jnp.bfloat16)
        for which in range(CORES):

            @pl.when(core == which)
            def _():
                for i in range(groups):
                    to = end + CORES * count * i + count * which
                    out_ref[to : to + count, :] = rows_ref[:, LANES * i : LANES * (i + 1)]

    for out_ref, which in ((kept_ref, core), (sent_ref, 1 - core)):
        for i in range(groups):
            out_ref[part * i : part * (i + 1), :] = x_ref[which, :, LANES * i : LANES * (i + 1)]
        for i in range(inv_groups):
            high, low = split(inv_ref[which, :, LANES * i : LANES * (i + 1)])
            out_ref[base + part * i : base + part * (i + 1), :] = high
            out_ref[shift + part * i : shift + part * (i + 1), :] = low


VMEM = pl.BlockSpec(memory_space=pltpu.VMEM)
SMALL = pltpu.CompilerParams(vmem_limit_bytes=4 * 2**20)


def prep(x, inverse, rows):
    total = (x.size // CORES + 2 * inverse.size // CORES + CORES * rows.size) // LANES
    out = jax.ShapeDtypeStruct((total, LANES), jnp.bfloat16)
    return pl.pallas_call(
        prep_body,
        in_specs=[VMEM, VMEM, VMEM],
        out_specs=[VMEM, VMEM],
        out_shape=[out, out],
        compiler_params=SMALL,
        name="prep",
    )(x, inverse, rows)


def owner_of(panel_ref):
    blocks = panel_ref.shape[1]
    at = lax.broadcasted_iota(jnp.int32, (1, blocks), 1)
    found = jnp.where(panel_ref[...] == blocks // 4, at, 0).astype(jnp.float32)
    return jnp.sum(found).astype(jnp.int32)


def first_body(panel_ref, kept_ref, got_ref, out_ref, later_ref):
    chips, length, _ = out_ref.shape
    per_chip = length // 2
    total = chips * per_chip
    core = lax.axis_index("core")
    kept = owner_of(panel_ref) % CORES == core
    out_ref[:, :per_chip, :] = jnp.where(kept, kept_ref[:total], got_ref[:total]).reshape(chips, per_chip, LANES)
    for n in range(2):
        at = pl.ds(pl.multiple_of(total + (2 * core + n) * per_chip, per_chip), per_chip)
        rows = (kept_ref[at, :].astype(jnp.float32) + got_ref[at, :].astype(jnp.float32)).astype(jnp.bfloat16)
        if n == 0:
            out_ref[:, per_chip:, :] = jnp.broadcast_to(rows[None], (chips, per_chip, LANES))
        else:
            later_ref[...] = rows


def first_operand(panel, kept, got, chips, per_chip):
    return pl.pallas_call(
        first_body,
        in_specs=[VMEM, VMEM, VMEM],
        out_specs=[VMEM, VMEM],
        out_shape=[
            jax.ShapeDtypeStruct((chips, 2 * per_chip, LANES), jnp.bfloat16),
            jax.ShapeDtypeStruct((per_chip, LANES), jnp.bfloat16),
        ],
        compiler_params=SMALL,
        name="first_operand",
    )(panel, kept, got)


def second_body(panel_ref, came_ref, rows_ref, out_ref):
    chips, length, _ = out_ref.shape
    per_chip = length // 2
    piece = came_ref[owner_of(panel_ref) // CORES, :per_chip, :]
    out_ref[:, :per_chip, :] = jnp.broadcast_to(piece[None], (chips, per_chip, LANES))
    out_ref[:, per_chip:, :] = jnp.broadcast_to(rows_ref[...][None], (chips, per_chip, LANES))


def second_operand(panel, came, rows):
    return pl.pallas_call(
        second_body,
        in_specs=[VMEM, VMEM, VMEM],
        out_specs=VMEM,
        out_shape=jax.ShapeDtypeStruct(came.shape, came.dtype),
        compiler_params=SMALL,
        name="second_operand",
    )(panel, came, rows)


def third_body(came_ref, out_ref):
    per_chip = came_ref.shape[1] // 2
    piece = came_ref[:, :per_chip, :].reshape(out_ref.shape[1:])
    for q in range(out_ref.shape[0]):
        out_ref[q] = piece


def third_operand(came, row_count):
    chips, length, _ = came.shape
    return pl.pallas_call(
        third_body,
        in_specs=[VMEM],
        out_specs=VMEM,
        out_shape=jax.ShapeDtypeStruct((row_count, chips * length // 2, LANES), came.dtype),
        compiler_params=SMALL,
        name="third_operand",
    )(came)


def triple(ref, rows, at, values, swapped):
    high, low = split(values)
    width = values.shape[1]
    for i, part in enumerate((high, low, high) if swapped else (high, high, low)):
        ref[rows, at + width * i : at + width * (i + 1)] = part


def unpack(got_ref, x_ref, inverse_ref):
    count, width = x_ref.shape
    quarters = got_ref.shape[0]
    part = count // quarters
    groups, inv_groups = width // LANES, inverse_ref.shape[1] // (3 * LANES)
    each = inv_groups // 2
    for q in range(quarters):
        to = slice(part * q, part * (q + 1))
        for i in range(groups):
            x_ref[to, LANES * i : LANES * (i + 1)] = got_ref[q, part * i : part * (i + 1), :]
        for n in range(2):
            for i in range(inv_groups):
                at = part * (groups + n * inv_groups + i)
                block = got_ref[q, at : at + part, :]
                for place in (0, 2) if n == 0 else (1,):
                    lane = LANES * (each * (3 * (i // each) + place) + i % each)
                    inverse_ref[to, lane : lane + LANES] = block


def kernel_half(x_ref, cols_ref, col_norm_ref, rows_own_ref, rows_other_ref, row_norm_ref, to_cols_ref, to_rows_ref,
                gram_ref, norm_ref, inv_ref):
    count, width = x_ref.shape
    size, half = rows_own_ref.shape
    core = lax.axis_index("core")
    wide = x_ref[...].astype(jnp.float32)
    norm = jnp.sqrt(jnp.sum(wide * wide, axis=1, keepdims=True) + 1e-06)
    norm = jnp.broadcast_to(norm, (count, LANES)).T
    norm_ref[...] = norm[:STEP]
    inv_ref[...] = 1.0 / norm[:STEP]
    own = pl.ds(pl.multiple_of(core * half, half), half)
    theirs = pl.ds(pl.multiple_of((1 - core) * half, half), half)
    for side, (from_norm_ref, to_ref) in enumerate(((col_norm_ref, to_cols_ref), (row_norm_ref, to_rows_ref))):
        if side == 0:
            gram_ref[...] = dot_t(cols_ref[...], x_ref[...])
        else:
            gram_ref[...] = dot_t(rows_own_ref[...], x_ref[:, own]) + dot_t(rows_other_ref[...], x_ref[:, theirs])

        @pl.loop(0, size // STEP)
        def _(i):
            at = pl.ds(pl.multiple_of(i * STEP, STEP), STEP)
            norm = jnp.concatenate([from_norm_ref[at, :]] * (count // LANES), axis=1)
            cosine = gram_ref[at, :] * (1.0 / norm) * inv_ref[...]
            values = layers(jnp.clip(cosine, -1.0, 1.0)) * (norm * norm_ref[...])
            triple(to_ref, at, 0, values, False)


def half_body(cols_ref, rows_own_ref, rows_other_ref, mine_hbm,
              col_norm_ref, row_norm_ref, to_cols_ref, to_rows_ref, inverse_ref,
              x_ref, gram_ref, norm_ref, inv_ref, mine_ref, sem):
    copy = pltpu.make_async_copy(mine_hbm, mine_ref, sem)
    copy.start()
    for pieces, to_ref in (((cols_ref,), col_norm_ref), ((rows_own_ref, rows_other_ref), row_norm_ref)):

        @pl.loop(0, to_ref.shape[0] // STEP)
        def _(i):
            at = pl.ds(pl.multiple_of(i * STEP, STEP), STEP)
            total = 1e-06
            for piece_ref in pieces:
                wide = piece_ref[at, :].astype(jnp.float32)
                total += jnp.sum(wide * wide, axis=1, keepdims=True)
            to_ref[at, :] = jnp.broadcast_to(jnp.sqrt(total), (STEP, LANES))

    copy.wait()
    unpack(mine_ref, x_ref, inverse_ref)
    kernel_half(x_ref, cols_ref, col_norm_ref, rows_own_ref, rows_other_ref, row_norm_ref, to_cols_ref, to_rows_ref,
                gram_ref, norm_ref, inv_ref)


def half_scratch(size, width):
    count = size // CORES
    return [pltpu.VMEM((count, width), jnp.bfloat16), pltpu.VMEM((size, count), jnp.float32)] + [
        pltpu.VMEM((STEP, count), jnp.float32)
    ] * 2


def half_step(cols, rows_own, rows_other, mine):
    size, width = cols.shape
    values = jax.ShapeDtypeStruct((size, 3 * size // CORES), jnp.bfloat16)
    norm = jax.ShapeDtypeStruct((size, LANES), jnp.float32)
    return pl.pallas_call(
        half_body,
        in_specs=[VMEM] * 3 + [pl.BlockSpec(memory_space=pl.ANY)],
        out_specs=[VMEM] * 5,
        out_shape=[norm, norm, values, values, jax.ShapeDtypeStruct((size // CORES, 3 * size), jnp.bfloat16)],
        scratch_shapes=half_scratch(size, width) + [pltpu.VMEM(mine.shape, mine.dtype), pltpu.SemaphoreType.DMA],
        compiler_params=pltpu.CompilerParams(vmem_limit_bytes=9 * 2**20),
        cost_estimate=pl.CostEstimate(
            flops=2 * size * size * width, bytes_accessed=8 * 2**20, transcendentals=6 * size * size
        ),
        name="half_step",
    )(cols, rows_own, rows_other, mine)


def update_body(panel_ref, cols_ref, col_norm_ref, rows_own_ref, rows_other_ref, row_norm_ref, own_cols_ref, own_rows_ref,
                own_inverse_ref, other_ref, trailing_ref, out_ref,
                x_ref, gram_ref, norm_ref, inv_ref, other_cols_ref, other_rows_ref, other_inverse_ref,
                k_cols_ref, k_rows_ref, inverse_ref, left_ref, right_ref):
    count, thrice = other_inverse_ref.shape
    core = lax.axis_index("core")
    unpack(other_ref, x_ref, other_inverse_ref)
    kernel_half(x_ref, cols_ref, col_norm_ref, rows_own_ref, rows_other_ref, row_norm_ref, other_cols_ref, other_rows_ref,
                gram_ref, norm_ref, inv_ref)
    each = thrice // 2
    for which, cols_of, rows_of, inverse_of in (
        (core, own_cols_ref, own_rows_ref, own_inverse_ref),
        (1 - core, other_cols_ref, other_rows_ref, other_inverse_ref),
    ):
        lanes = pl.ds(pl.multiple_of(which * each, each), each)
        k_cols_ref[:, lanes] = cols_of[...]
        k_rows_ref[:, lanes] = rows_of[...]
        inverse_ref[pl.ds(pl.multiple_of(which * count, count), count), :] = inverse_of[...]
    for k_ref, to_ref, swapped in ((k_cols_ref, right_ref, True), (k_rows_ref, left_ref, False)):
        every = slice(0, k_ref.shape[0])
        triple(to_ref, every, 0, dot_t(k_ref[:, :each], inverse_ref[:count, :each]), swapped)
        triple(to_ref, every, each, dot_t(k_ref[...], inverse_ref[count:, :]), swapped)
    blocks = panel_ref.shape[1]
    here = lax.broadcasted_iota(jnp.int32, (1, blocks), 1) == CORES * lax.axis_index("chip") + core
    own_rank = jnp.sum(jnp.where(here, panel_ref[...], 0).astype(jnp.float32))
    old = trailing_ref[...]
    out_ref[...] = jnp.where(own_rank > blocks // 4, old - dot_t(left_ref[...], right_ref[...]), old)


def update(panel, cols, rows_own, rows_other, mine, other, trailing):
    size, width = cols.shape
    col_norm, row_norm, *own = half_step(cols, rows_own, rows_other, mine)
    values = pltpu.VMEM((size, 3 * size // CORES), jnp.bfloat16)
    whole = pltpu.VMEM((size, 3 * size), jnp.bfloat16)
    return pl.pallas_call(
        update_body,
        in_specs=[VMEM] * 11,
        out_specs=VMEM,
        out_shape=jax.ShapeDtypeStruct(trailing.shape, trailing.dtype),
        scratch_shapes=half_scratch(size, width)
        + [values] * 2
        + [pltpu.VMEM((size // CORES, 3 * size), jnp.bfloat16)]
        + [whole] * 5,
        compiler_params=pltpu.CompilerParams(vmem_limit_bytes=20 * 2**20),
        name="update",
    )(panel, cols, col_norm, rows_own, rows_other, row_norm, *own, other, trailing)


def on_device(chips, row_count, panel, centres_cols, centres_rows, diag_inverse, trailing):
    size, width = centres_cols.shape
    part = size // (CORES * row_count)
    half = width // CORES
    row = lax.axis_index("row")
    panel = panel[None]
    swap = [(0, 1), (1, 0)]

    def parts(block):
        return lax.dynamic_index_in_dim(block.reshape(CORES, row_count, part, -1), row, 1, keepdims=False)

    kept, sent = prep(parts(centres_cols), parts(diag_inverse), centres_rows)
    got = lax.ppermute(sent, "core", swap)
    per_chip = part * (width + 2 * size) // (LANES * chips)
    outgoing, rows_later = first_operand(panel, kept, got, chips, per_chip)
    first = lax.all_to_all(outgoing, "chip", 0, 0)
    second = lax.all_to_all(second_operand(panel, first, rows_later), "chip", 0, 0)
    all_mine = lax.all_to_all(third_operand(second, row_count), "row", 0, 0)

    tiles = [came[:, i : i + 8] for came in (first, second) for i in range(per_chip, 2 * per_chip, 8)]
    rows_own = jnp.concatenate([tile.reshape(size, LANES) for tile in tiles], axis=1)
    rows_other = lax.ppermute(rows_own, "core", swap)
    all_mine, rows_other = lax.optimization_barrier((all_mine, rows_other))
    all_other = lax.ppermute(all_mine, "core", swap)
    return update(panel, centres_cols, rows_own, rows_other, all_mine, all_other, trailing)


def solution(mesh):
    col_count, row_count = mesh.devices.shape
    chips = col_count // CORES
    fine = Mesh(mesh.devices.reshape(chips, CORES, row_count), ("chip", "core", "row"))

    def step(*arrays):
        return on_device(chips, row_count, *arrays)

    col = ("chip", "core")
    return jax.shard_map(
        step,
        mesh=fine,
        in_specs=(P(), P(col, None), P(("row",) + col, None), P(col, None), P("row", col)),
        out_specs=P("row", col),
        check_vma=False,
    )
```

```python
import math

import jax
import jax.numpy as jnp
from jax import lax
from jax.experimental import pallas as pl
from jax.experimental.pallas import tpu as pltpu
from jax.sharding import Mesh, PartitionSpec as P

LAYERS = 3
CORES = 2
LANES = 128
STEP = 128
WIDE = (0.4999999720071538, -0.06830646500676399, 0.028277340639243406, -0.01566003030791659,
        0.008837209300279753, -0.003820798788545866, 0.0008313362870811599)
NARROW = (0.4999769000530011, -0.06803611787881512, 0.026989768593852003, -0.012483028758839653,
          0.004564983607401579, -0.0008544733222650566)


def repeat_gather(piece, axis, count):
    return lax.all_to_all(jnp.broadcast_to(piece[None], (count,) + piece.shape), axis, 0, 0)


def split(values):
    high = values.astype(jnp.bfloat16)
    return high, (values - high.astype(jnp.float32)).astype(jnp.bfloat16)


def dot_t(left, right):
    return lax.dot_general(left, right, (((1,), (1,)), ((), ())), preferred_element_type=jnp.float32)


def poly(x, coefs):
    total = coefs[-1]
    for coef in coefs[-2::-1]:
        total = total * x + coef
    return total


def layers(rho):
    theta = rho
    for layer in range(LAYERS):
        size = jnp.abs(rho) if layer == 0 else rho
        rest = jnp.maximum(1.0 - size, 1e-30)
        below = rest * lax.rsqrt(rest)
        above = 1.0 + size
        above = above * lax.rsqrt(above) * (1.0 / math.pi)
        angle = below * poly(size, NARROW if layer == 2 else WIDE)
        zero_order = 1.0 - angle
        if layer == 0:
            zero_order = jnp.where(rho < 0.0, angle, zero_order)
        rho_next = below * above + zero_order * rho
        theta = theta * zero_order + rho_next
        rho = rho_next
    return theta


def prep_body(x_ref, inv_ref, rows_ref, kept_ref, sent_ref):
    core = lax.axis_index("core")
    _, part, width = x_ref.shape
    groups, inv_groups = width // LANES, inv_ref.shape[2] // LANES
    base = part * groups
    shift = base + part * inv_groups
    end = shift + part * inv_groups
    count = rows_ref.shape[0]
    for out_ref in (kept_ref, sent_ref):
        out_ref[end:, :] = jnp.zeros((kept_ref.shape[0] - end, LANES), jnp.bfloat16)
        for which in range(CORES):

            @pl.when(core == which)
            def _():
                for i in range(groups):
                    to = end + CORES * count * i + count * which
                    out_ref[to : to + count, :] = rows_ref[:, LANES * i : LANES * (i + 1)]

    for out_ref, which in ((kept_ref, core), (sent_ref, 1 - core)):
        for i in range(groups):
            out_ref[part * i : part * (i + 1), :] = x_ref[which, :, LANES * i : LANES * (i + 1)]
        for i in range(inv_groups):
            high, low = split(inv_ref[which, :, LANES * i : LANES * (i + 1)])
            out_ref[base + part * i : base + part * (i + 1), :] = high
            out_ref[shift + part * i : shift + part * (i + 1), :] = low


VMEM = pl.BlockSpec(memory_space=pltpu.VMEM)
SMALL = pltpu.CompilerParams(vmem_limit_bytes=4 * 2**20)


def prep(x, inverse, rows):
    total = (x.size // CORES + 2 * inverse.size // CORES + CORES * rows.size) // LANES
    out = jax.ShapeDtypeStruct((total, LANES), jnp.bfloat16)
    return pl.pallas_call(
        prep_body,
        in_specs=[VMEM, VMEM, VMEM],
        out_specs=[VMEM, VMEM],
        out_shape=[out, out],
        compiler_params=SMALL,
        name="prep",
    )(x, inverse, rows)


def owner_of(panel_ref):
    blocks = panel_ref.shape[1]
    at = lax.broadcasted_iota(jnp.int32, (1, blocks), 1)
    found = jnp.where(panel_ref[...] == blocks // 4, at, 0).astype(jnp.float32)
    return jnp.sum(found).astype(jnp.int32)


def first_body(panel_ref, kept_ref, got_ref, out_ref, rows_ref):
    total = out_ref.shape[0] * out_ref.shape[1]
    count = rows_ref.shape[0]
    core = lax.axis_index("core")
    kept = owner_of(panel_ref) % CORES == core
    out_ref[...] = jnp.where(kept, kept_ref[:total], got_ref[:total]).reshape(out_ref.shape)
    at = pl.ds(pl.multiple_of(total + core * count, count), count)
    rows_ref[...] = (kept_ref[at, :].astype(jnp.float32) + got_ref[at, :].astype(jnp.float32)).astype(jnp.bfloat16)


def first_operand(panel, kept, got, chips, per_chip):
    count = (kept.shape[0] - chips * per_chip) // CORES
    return pl.pallas_call(
        first_body,
        in_specs=[VMEM, VMEM, VMEM],
        out_specs=[VMEM, VMEM],
        out_shape=[
            jax.ShapeDtypeStruct((chips, per_chip, LANES), jnp.bfloat16),
            jax.ShapeDtypeStruct((count, LANES), jnp.bfloat16),
        ],
        compiler_params=SMALL,
        name="first_operand",
    )(panel, kept, got)


def second_body(panel_ref, came_ref, rows_ref, out_ref):
    chips, per_chip, _ = came_ref.shape
    piece = came_ref[owner_of(panel_ref) // CORES]
    out_ref[:, :per_chip, :] = jnp.broadcast_to(piece[None], (chips, per_chip, LANES))
    out_ref[:, per_chip:, :] = jnp.broadcast_to(rows_ref[...][None], (chips,) + rows_ref.shape)


def second_operand(panel, came, rows):
    chips, per_chip, _ = came.shape
    return pl.pallas_call(
        second_body,
        in_specs=[VMEM, VMEM, VMEM],
        out_specs=VMEM,
        out_shape=jax.ShapeDtypeStruct((chips, per_chip + rows.shape[0], LANES), came.dtype),
        compiler_params=SMALL,
        name="second_operand",
    )(panel, came, rows)


def third_body(came_ref, out_ref):
    per_chip = out_ref.shape[1] // came_ref.shape[0]
    piece = came_ref[:, :per_chip, :].reshape(out_ref.shape[1:])
    for q in range(out_ref.shape[0]):
        out_ref[q] = piece


def third_operand(came, row_count, per_chip):
    return pl.pallas_call(
        third_body,
        in_specs=[VMEM],
        out_specs=VMEM,
        out_shape=jax.ShapeDtypeStruct((row_count, came.shape[0] * per_chip, LANES), came.dtype),
        compiler_params=SMALL,
        name="third_operand",
    )(came)


def triple(ref, rows, at, values, swapped):
    high, low = split(values)
    width = values.shape[1]
    for i, part in enumerate((high, low, high) if swapped else (high, high, low)):
        ref[rows, at + width * i : at + width * (i + 1)] = part


def unpack(got_ref, x_ref, inverse_ref):
    count, width = x_ref.shape
    quarters = got_ref.shape[0]
    part = count // quarters
    groups, inv_groups = width // LANES, inverse_ref.shape[1] // (3 * LANES)
    each = inv_groups // 2
    for q in range(quarters):
        to = slice(part * q, part * (q + 1))
        for i in range(groups):
            x_ref[to, LANES * i : LANES * (i + 1)] = got_ref[q, part * i : part * (i + 1), :]
        for n in range(2):
            for i in range(inv_groups):
                at = part * (groups + n * inv_groups + i)
                block = got_ref[q, at : at + part, :]
                for place in (0, 2) if n == 0 else (1,):
                    lane = LANES * (each * (3 * (i // each) + place) + i % each)
                    inverse_ref[to, lane : lane + LANES] = block


def kernel_half(x_ref, cols_ref, col_norm_ref, rows_own_ref, rows_other_ref, row_norm_ref, to_cols_ref, to_rows_ref,
                gram_ref, norm_ref, inv_ref):
    count, width = x_ref.shape
    size, half = rows_own_ref.shape
    core = lax.axis_index("core")
    wide = x_ref[...].astype(jnp.float32)
    norm = jnp.sqrt(jnp.sum(wide * wide, axis=1, keepdims=True) + 1e-06)
    norm = jnp.broadcast_to(norm, (count, LANES)).T
    norm_ref[...] = norm[:STEP]
    inv_ref[...] = 1.0 / norm[:STEP]
    own = pl.ds(pl.multiple_of(core * half, half), half)
    theirs = pl.ds(pl.multiple_of((1 - core) * half, half), half)
    for side, (from_norm_ref, to_ref) in enumerate(((col_norm_ref, to_cols_ref), (row_norm_ref, to_rows_ref))):
        if side == 0:
            gram_ref[...] = dot_t(cols_ref[...], x_ref[...])
        else:
            gram_ref[...] = dot_t(rows_own_ref[...], x_ref[:, own]) + dot_t(rows_other_ref[...], x_ref[:, theirs])

        @pl.loop(0, size // STEP)
        def _(i):
            at = pl.ds(pl.multiple_of(i * STEP, STEP), STEP)
            norm = jnp.concatenate([from_norm_ref[at, :]] * (count // LANES), axis=1)
            cosine = gram_ref[at, :] * (1.0 / norm) * inv_ref[...]
            values = layers(jnp.clip(cosine, -1.0, 1.0)) * (norm * norm_ref[...])
            triple(to_ref, at, 0, values, False)


def half_body(cols_ref, rows_own_ref, rows_other_ref, mine_hbm,
              col_norm_ref, row_norm_ref, to_cols_ref, to_rows_ref, inverse_ref,
              x_ref, gram_ref, norm_ref, inv_ref, mine_ref, sem):
    copy = pltpu.make_async_copy(mine_hbm, mine_ref, sem)
    copy.start()
    for pieces, to_ref in (((cols_ref,), col_norm_ref), ((rows_own_ref, rows_other_ref), row_norm_ref)):

        @pl.loop(0, to_ref.shape[0] // STEP)
        def _(i):
            at = pl.ds(pl.multiple_of(i * STEP, STEP), STEP)
            total = 1e-06
            for piece_ref in pieces:
                wide = piece_ref[at, :].astype(jnp.float32)
                total += jnp.sum(wide * wide, axis=1, keepdims=True)
            to_ref[at, :] = jnp.broadcast_to(jnp.sqrt(total), (STEP, LANES))

    copy.wait()
    unpack(mine_ref, x_ref, inverse_ref)
    kernel_half(x_ref, cols_ref, col_norm_ref, rows_own_ref, rows_other_ref, row_norm_ref, to_cols_ref, to_rows_ref,
                gram_ref, norm_ref, inv_ref)


def half_scratch(size, width):
    count = size // CORES
    return [pltpu.VMEM((count, width), jnp.bfloat16), pltpu.VMEM((size, count), jnp.float32)] + [
        pltpu.VMEM((STEP, count), jnp.float32)
    ] * 2


def half_step(cols, rows_own, rows_other, mine):
    size, width = cols.shape
    values = jax.ShapeDtypeStruct((size, 3 * size // CORES), jnp.bfloat16)
    norm = jax.ShapeDtypeStruct((size, LANES), jnp.float32)
    return pl.pallas_call(
        half_body,
        in_specs=[VMEM] * 3 + [pl.BlockSpec(memory_space=pl.ANY)],
        out_specs=[VMEM] * 5,
        out_shape=[norm, norm, values, values, jax.ShapeDtypeStruct((size // CORES, 3 * size), jnp.bfloat16)],
        scratch_shapes=half_scratch(size, width) + [pltpu.VMEM(mine.shape, mine.dtype), pltpu.SemaphoreType.DMA],
        compiler_params=pltpu.CompilerParams(vmem_limit_bytes=9 * 2**20),
        cost_estimate=pl.CostEstimate(
            flops=2 * size * size * width, bytes_accessed=8 * 2**20, transcendentals=6 * size * size
        ),
        name="half_step",
    )(cols, rows_own, rows_other, mine)


def update_body(panel_ref, cols_ref, col_norm_ref, rows_own_ref, rows_other_ref, row_norm_ref, own_cols_ref, own_rows_ref,
                own_inverse_ref, other_ref, trailing_ref, out_ref,
                x_ref, gram_ref, norm_ref, inv_ref, other_cols_ref, other_rows_ref, other_inverse_ref,
                k_cols_ref, k_rows_ref, inverse_ref, left_ref, right_ref):
    count, thrice = other_inverse_ref.shape
    core = lax.axis_index("core")
    unpack(other_ref, x_ref, other_inverse_ref)
    kernel_half(x_ref, cols_ref, col_norm_ref, rows_own_ref, rows_other_ref, row_norm_ref, other_cols_ref, other_rows_ref,
                gram_ref, norm_ref, inv_ref)
    each = thrice // 2
    for which, cols_of, rows_of, inverse_of in (
        (core, own_cols_ref, own_rows_ref, own_inverse_ref),
        (1 - core, other_cols_ref, other_rows_ref, other_inverse_ref),
    ):
        lanes = pl.ds(pl.multiple_of(which * each, each), each)
        k_cols_ref[:, lanes] = cols_of[...]
        k_rows_ref[:, lanes] = rows_of[...]
        inverse_ref[pl.ds(pl.multiple_of(which * count, count), count), :] = inverse_of[...]
    for k_ref, to_ref, swapped in ((k_cols_ref, right_ref, True), (k_rows_ref, left_ref, False)):
        every = slice(0, k_ref.shape[0])
        triple(to_ref, every, 0, dot_t(k_ref[:, :each], inverse_ref[:count, :each]), swapped)
        triple(to_ref, every, each, dot_t(k_ref[...], inverse_ref[count:, :]), swapped)
    blocks = panel_ref.shape[1]
    here = lax.broadcasted_iota(jnp.int32, (1, blocks), 1) == CORES * lax.axis_index("chip") + core
    own_rank = jnp.sum(jnp.where(here, panel_ref[...], 0).astype(jnp.float32))
    old = trailing_ref[...]
    out_ref[...] = jnp.where(own_rank > blocks // 4, old - dot_t(left_ref[...], right_ref[...]), old)


def update(panel, cols, rows_own, rows_other, mine, other, trailing):
    size, width = cols.shape
    col_norm, row_norm, *own = half_step(cols, rows_own, rows_other, mine)
    values = pltpu.VMEM((size, 3 * size // CORES), jnp.bfloat16)
    whole = pltpu.VMEM((size, 3 * size), jnp.bfloat16)
    return pl.pallas_call(
        update_body,
        in_specs=[VMEM] * 11,
        out_specs=VMEM,
        out_shape=jax.ShapeDtypeStruct(trailing.shape, trailing.dtype),
        scratch_shapes=half_scratch(size, width)
        + [values] * 2
        + [pltpu.VMEM((size // CORES, 3 * size), jnp.bfloat16)]
        + [whole] * 5,
        compiler_params=pltpu.CompilerParams(vmem_limit_bytes=20 * 2**20),
        name="update",
    )(panel, cols, col_norm, rows_own, rows_other, row_norm, *own, other, trailing)


def on_device(chips, row_count, panel, centres_cols, centres_rows, diag_inverse, trailing):
    size, width = centres_cols.shape
    part = size // (CORES * row_count)
    half = width // CORES
    row = lax.axis_index("row")
    panel = panel[None]
    swap = [(0, 1), (1, 0)]

    def parts(block):
        return lax.dynamic_index_in_dim(block.reshape(CORES, row_count, part, -1), row, 1, keepdims=False)

    kept, sent = prep(parts(centres_cols), parts(diag_inverse), centres_rows)
    got = lax.ppermute(sent, "core", swap)
    per_chip = part * (width + 2 * size) // (LANES * chips)
    outgoing, rows_chip = first_operand(panel, kept, got, chips, per_chip)
    first = lax.all_to_all(outgoing, "chip", 0, 0)
    second = lax.all_to_all(second_operand(panel, first, rows_chip), "chip", 0, 0)
    all_mine = lax.all_to_all(third_operand(second, row_count, per_chip), "row", 0, 0)

    tiles = [second[:, i : i + 8] for i in range(per_chip, second.shape[1], 8)]
    rows_own = jnp.concatenate([tile.reshape(size, LANES) for tile in tiles], axis=1)
    rows_other = lax.ppermute(rows_own, "core", swap)
    all_mine, rows_other = lax.optimization_barrier((all_mine, rows_other))
    all_other = lax.ppermute(all_mine, "core", swap)
    return update(panel, centres_cols, rows_own, rows_other, all_mine, all_other, trailing)


def solution(mesh):
    col_count, row_count = mesh.devices.shape
    chips = col_count // CORES
    fine = Mesh(mesh.devices.reshape(chips, CORES, row_count), ("chip", "core", "row"))

    def step(*arrays):
        return on_device(chips, row_count, *arrays)

    col = ("chip", "core")
    return jax.shard_map(
        step,
        mesh=fine,
        in_specs=(P(), P(col, None), P(("row",) + col, None), P(col, None), P("row", col)),
        out_specs=P("row", col),
        check_vma=False,
    )
```

```python
import math

import jax
import jax.numpy as jnp
from jax import lax
from jax.experimental import pallas as pl
from jax.experimental.pallas import tpu as pltpu
from jax.sharding import Mesh, PartitionSpec as P

LAYERS = 3
CORES = 2
LANES = 128
STEP = 64
WIDE = (0.4999999720071538, -0.06830646500676399, 0.028277340639243406, -0.01566003030791659,
        0.008837209300279753, -0.003820798788545866, 0.0008313362870811599)
NARROW = (0.4999769000530011, -0.06803611787881512, 0.026989768593852003, -0.012483028758839653,
          0.004564983607401579, -0.0008544733222650566)


def repeat_gather(piece, axis, count):
    return lax.all_to_all(jnp.broadcast_to(piece[None], (count,) + piece.shape), axis, 0, 0)


def split(values):
    high = values.astype(jnp.bfloat16)
    return high, (values - high.astype(jnp.float32)).astype(jnp.bfloat16)


def dot_t(left, right):
    return lax.dot_general(left, right, (((1,), (1,)), ((), ())), preferred_element_type=jnp.float32)


def poly(x, coefs):
    total = coefs[-1]
    for coef in coefs[-2::-1]:
        total = total * x + coef
    return total


def layers(rho):
    theta = rho
    for layer in range(LAYERS):
        size = jnp.abs(rho) if layer == 0 else rho
        rest = jnp.maximum(1.0 - size, 1e-30)
        below = rest * lax.rsqrt(rest)
        above = 1.0 + size
        above = above * lax.rsqrt(above) * (1.0 / math.pi)
        angle = below * poly(size, NARROW if layer == 2 else WIDE)
        zero_order = 1.0 - angle
        if layer == 0:
            zero_order = jnp.where(rho < 0.0, angle, zero_order)
        rho_next = below * above + zero_order * rho
        theta = theta * zero_order + rho_next
        rho = rho_next
    return theta


def prep_body(panel_ref, x_ref, inv_ref, rows_ref, kept_ref, sent_ref):
    core = lax.axis_index("core")
    size, width = x_ref.shape
    half, groups = width // CORES, inv_ref.shape[1] // LANES
    rows = size // CORES
    base = size * (half // LANES)
    end = base + 2 * rows * groups
    count = rows_ref.shape[0]
    for out_ref in (kept_ref, sent_ref):
        out_ref[end:, :] = jnp.zeros((kept_ref.shape[0] - end, LANES), jnp.bfloat16)
        for which in range(CORES):

            @pl.when(core == which)
            def _():
                for i in range(width // LANES):
                    to = end + CORES * count * i + count * which
                    out_ref[to : to + count, :] = rows_ref[:, LANES * i : LANES * (i + 1)]

    for out_ref, which in ((kept_ref, core), (sent_ref, 1 - core)):
        for i in range(half // LANES):
            at = pl.multiple_of(which * half + LANES * i, LANES)
            out_ref[size * i : size * (i + 1), :] = x_ref[:, pl.ds(at, LANES)]
    for out_ref, which in ((kept_ref, core), (sent_ref, 1 - core)):
        for i in range(groups):
            at = pl.multiple_of(which * rows, rows)
            high, low = split(inv_ref[pl.ds(at, rows), LANES * i : LANES * (i + 1)])
            out_ref[base + rows * i : base + rows * (i + 1), :] = high
            shift = base + rows * groups
            out_ref[shift + rows * i : shift + rows * (i + 1), :] = low


VMEM = pl.BlockSpec(memory_space=pltpu.VMEM)
SMALL = pltpu.CompilerParams(vmem_limit_bytes=4 * 2**20)


def prep(panel, x, inverse, rows):
    size, width = x.shape
    total = (width * size // CORES + 2 * inverse.size // CORES + CORES * rows.size) // LANES
    out = jax.ShapeDtypeStruct((total, LANES), jnp.bfloat16)
    return pl.pallas_call(
        prep_body,
        in_specs=[VMEM] * 4,
        out_specs=[VMEM, VMEM],
        out_shape=[out, out],
        compiler_params=SMALL,
        name="prep",
    )(panel, x, inverse, rows)


def owner_of(panel_ref):
    blocks = panel_ref.shape[1]
    at = lax.broadcasted_iota(jnp.int32, (1, blocks), 1)
    found = jnp.where(panel_ref[...] == blocks // 4, at, 0).astype(jnp.float32)
    return jnp.sum(found).astype(jnp.int32)


def first_body(panel_ref, kept_ref, got_ref, out_ref, rows_ref):
    total = out_ref.shape[0] * out_ref.shape[1]
    count = rows_ref.shape[0]
    core = lax.axis_index("core")
    kept = owner_of(panel_ref) % CORES == core
    out_ref[...] = jnp.where(kept, kept_ref[:total], got_ref[:total]).reshape(out_ref.shape)
    at = pl.ds(pl.multiple_of(total + core * count, count), count)
    rows_ref[...] = (kept_ref[at, :].astype(jnp.float32) + got_ref[at, :].astype(jnp.float32)).astype(jnp.bfloat16)


def first_operand(panel, kept, got, chips, per_chip):
    count = (kept.shape[0] - chips * per_chip) // CORES
    return pl.pallas_call(
        first_body,
        in_specs=[VMEM, VMEM, VMEM],
        out_specs=[VMEM, VMEM],
        out_shape=[
            jax.ShapeDtypeStruct((chips, per_chip, LANES), jnp.bfloat16),
            jax.ShapeDtypeStruct((count, LANES), jnp.bfloat16),
        ],
        compiler_params=SMALL,
        name="first_operand",
    )(panel, kept, got)


def second_body(panel_ref, came_ref, rows_ref, out_ref):
    chips, per_chip, _ = came_ref.shape
    piece = came_ref[owner_of(panel_ref) // CORES]
    out_ref[:, :per_chip, :] = jnp.broadcast_to(piece[None], (chips, per_chip, LANES))
    out_ref[:, per_chip:, :] = jnp.broadcast_to(rows_ref[...][None], (chips,) + rows_ref.shape)


def second_operand(panel, came, rows):
    chips, per_chip, _ = came.shape
    return pl.pallas_call(
        second_body,
        in_specs=[VMEM, VMEM, VMEM],
        out_specs=VMEM,
        out_shape=jax.ShapeDtypeStruct((chips, per_chip + rows.shape[0], LANES), came.dtype),
        compiler_params=SMALL,
        name="second_operand",
    )(panel, came, rows)


def third_body(came_ref, out_ref):
    per_chip = out_ref.shape[1] // came_ref.shape[0]
    piece = came_ref[:, :per_chip, :].reshape(out_ref.shape[1:])
    for q in range(out_ref.shape[0]):
        out_ref[q] = piece


def third_operand(came, row_count, per_chip):
    return pl.pallas_call(
        third_body,
        in_specs=[VMEM],
        out_specs=VMEM,
        out_shape=jax.ShapeDtypeStruct((row_count, came.shape[0] * per_chip, LANES), came.dtype),
        compiler_params=SMALL,
        name="third_operand",
    )(came)


def triple(ref, rows, at, values, swapped):
    high, low = split(values)
    width = values.shape[1]
    for i, part in enumerate((high, low, high) if swapped else (high, high, low)):
        ref[rows, at + width * i : at + width * (i + 1)] = part


def unpack(got_ref, x_ref, inverse_ref, places):
    quarters = got_ref.shape[0]
    size, half = x_ref.shape
    quarter = size // quarters
    part = quarter // CORES
    groups, inv_groups = half // LANES, size // LANES
    each = inv_groups // 2
    for q in range(quarters):
        for i in range(groups):
            x_ref[quarter * q : quarter * (q + 1), LANES * i : LANES * (i + 1)] = got_ref[q, quarter * i : quarter * (i + 1), :]
        to = places[q]
        for n in range(2):
            for i in range(inv_groups):
                at = quarter * groups + (n * inv_groups + i) * part
                block = got_ref[q, at : at + part, :]
                for place in (0, 2) if n == 0 else (1,):
                    lane = LANES * (inv_groups * place + i)
                    inverse_ref[to : to + part, lane : lane + LANES] = block


def squares(x_ref):
    wide = x_ref[...].astype(jnp.float32)
    total = jnp.sum(wide * wide, axis=1, keepdims=True)
    return jnp.broadcast_to(total, (x_ref.shape[0], LANES)).T[:8]


def half_body(cols_ref, rows_own_ref, rows_other_ref, mine_hbm,
              col_norm_ref, row_norm_ref, gram_cols_ref, gram_rows_ref, square_ref, inverse_ref,
              x_ref, mine_ref, sem):
    copy = pltpu.make_async_copy(mine_hbm, mine_ref, sem)
    copy.start()
    for pieces, to_ref in (((cols_ref,), col_norm_ref), ((rows_own_ref, rows_other_ref), row_norm_ref)):

        @pl.loop(0, to_ref.shape[0] // LANES)
        def _(i):
            at = pl.ds(pl.multiple_of(i * LANES, LANES), LANES)
            total = 1e-06
            for piece_ref in pieces:
                wide = piece_ref[at, :].astype(jnp.float32)
                total += jnp.sum(wide * wide, axis=1, keepdims=True)
            to_ref[at, :] = jnp.broadcast_to(jnp.sqrt(total), (LANES, LANES))

    copy.wait()
    half, count = x_ref.shape[1], inverse_ref.shape[0]
    quarters = mine_ref.shape[0]
    unpack(mine_ref, x_ref, inverse_ref, [count // quarters * q for q in range(quarters)])
    own = pl.ds(pl.multiple_of(lax.axis_index("core") * half, half), half)
    gram_cols_ref[...] = dot_t(cols_ref[:, own], x_ref[...])
    gram_rows_ref[...] = dot_t(rows_own_ref[...], x_ref[...])
    square_ref[...] = squares(x_ref)


def half_step(cols, rows_own, rows_other, mine):
    size, width = cols.shape
    norm = jax.ShapeDtypeStruct((size, LANES), jnp.float32)
    square = jax.ShapeDtypeStruct((size, size), jnp.float32)
    return pl.pallas_call(
        half_body,
        in_specs=[VMEM] * 3 + [pl.BlockSpec(memory_space=pl.ANY)],
        out_specs=[VMEM] * 6,
        out_shape=[
            norm,
            norm,
            square,
            square,
            jax.ShapeDtypeStruct((8, size), jnp.float32),
            jax.ShapeDtypeStruct((size // CORES, 3 * size), jnp.bfloat16),
        ],
        scratch_shapes=[
            pltpu.VMEM((size, width // CORES), jnp.bfloat16),
            pltpu.VMEM(mine.shape, mine.dtype),
            pltpu.SemaphoreType.DMA,
        ],
        compiler_params=pltpu.CompilerParams(vmem_limit_bytes=9 * 2**20),
        cost_estimate=pl.CostEstimate(
            flops=4 * size * size * (width // CORES), bytes_accessed=8 * 2**20, transcendentals=0
        ),
        name="half_step",
    )(cols, rows_own, rows_other, mine)


def update_body(panel_ref, cols_ref, col_norm_ref, rows_ref, row_norm_ref, gram_cols_ref, gram_rows_ref, square_ref,
                inverse_own_ref, other_ref, trailing_ref, out_ref,
                x_ref, inverse_ref, gram_ref, gram_sum_ref, norm_ref, inv_ref, k_cols_ref, k_rows_ref, left_ref, right_ref):
    size, half = x_ref.shape
    core = lax.axis_index("core")
    quarters, count = other_ref.shape[0], inverse_own_ref.shape[0]
    pair, part = count // 2, count // quarters
    unpack(other_ref, x_ref, inverse_ref, [count * (q // 2) + pair + part * (q % 2) for q in range(quarters)])
    for n in range(2):
        inverse_ref[count * n : count * n + pair, :] = inverse_own_ref[pair * n : pair * (n + 1), :]
    norm = jnp.sqrt(square_ref[...] + squares(x_ref) + 1e-06)
    norm_ref[...] = jnp.concatenate([norm] * (STEP // 8), axis=0)
    inv_ref[...] = jnp.concatenate([1.0 / norm] * (STEP // 8), axis=0)

    def values_of(gram, from_norm, to_ref, at):
        norm = jnp.concatenate([from_norm] * (size // LANES), axis=1)
        cosine = gram * (1.0 / norm) * inv_ref[...]
        values = layers(jnp.clip(cosine, -1.0, 1.0)) * (norm * norm_ref[...])
        triple(to_ref, at, 0, values, False)

    theirs = pl.ds(pl.multiple_of((1 - core) * half, half), half)
    gram_ref[...] = gram_cols_ref[...] + dot_t(cols_ref[:, theirs], x_ref[...])
    n_steps = size // STEP

    def block(i, extent):
        return pl.ds(pl.multiple_of(i * extent, extent), extent)

    gram_sum_ref[...] = gram_rows_ref[...] + dot_t(rows_ref[...], x_ref[...])

    for gram, from_norm, k_ref, to_ref, swapped in (
        (gram_ref, col_norm_ref, k_cols_ref, right_ref, True),
        (gram_sum_ref, row_norm_ref, k_rows_ref, left_ref, False),
    ):

        @pl.loop(0, n_steps)
        def _(i):
            at = block(i, STEP)
            values_of(gram[at, :], from_norm[at, :], k_ref, at)

        triple(to_ref, slice(0, size), 0, dot_t(k_ref[...], inverse_ref[...]), swapped)

    blocks = panel_ref.shape[1]
    here = lax.broadcasted_iota(jnp.int32, (1, blocks), 1) == CORES * lax.axis_index("chip") + core
    own_rank = jnp.sum(jnp.where(here, panel_ref[...], 0).astype(jnp.float32))
    old = trailing_ref[...]
    out_ref[...] = jnp.where(own_rank > blocks // 4, old - dot_t(left_ref[...], right_ref[...]), old)


def update(panel, cols, rows_own, rows_other, mine, other, trailing):
    size, width = cols.shape
    col_norm, row_norm, gram_cols, gram_rows, square, inverse_own = half_step(cols, rows_own, rows_other, mine)
    thrice = pltpu.VMEM((size, 3 * size), jnp.bfloat16)
    lanes = pltpu.VMEM((STEP, size), jnp.float32)
    return pl.pallas_call(
        update_body,
        in_specs=[VMEM] * 11,
        out_specs=VMEM,
        out_shape=jax.ShapeDtypeStruct(trailing.shape, trailing.dtype),
        scratch_shapes=[pltpu.VMEM((size, width // CORES), jnp.bfloat16), thrice]
        + [pltpu.VMEM((size, size), jnp.float32)] * 2
        + [lanes] * 2
        + [thrice] * 4,
        compiler_params=pltpu.CompilerParams(vmem_limit_bytes=22 * 2**20),
        name="update",
    )(panel, cols, col_norm, rows_other, row_norm, gram_cols, gram_rows, square, inverse_own,
      other, trailing)


def on_device(chips, row_count, panel, centres_cols, centres_rows, diag_inverse, trailing):
    size, width = centres_cols.shape
    quarter = size // row_count
    row = lax.axis_index("row")
    panel = panel[None]
    swap = [(0, 1), (1, 0)]

    x = lax.dynamic_slice_in_dim(centres_cols, row * quarter, quarter, 0)
    inverse = lax.dynamic_slice_in_dim(diag_inverse, row * quarter, quarter, 0)
    kept, sent = prep(panel, x, inverse, centres_rows)
    got = lax.ppermute(sent, "core", swap)
    per_chip = (2 * width * quarter // CORES) // (LANES * chips)
    outgoing, rows_chip = first_operand(panel, kept, got, chips, per_chip)
    first = lax.all_to_all(outgoing, "chip", 0, 0)
    second = lax.all_to_all(second_operand(panel, first, rows_chip), "chip", 0, 0)
    all_mine = lax.all_to_all(third_operand(second, row_count, per_chip), "row", 0, 0)

    tiles = [second[:, i : i + 8] for i in range(per_chip, second.shape[1], 8)]
    rows_own = jnp.concatenate([tile.reshape(size, LANES) for tile in tiles], axis=1)
    rows_other = lax.ppermute(rows_own, "core", swap)
    all_mine, rows_other = lax.optimization_barrier((all_mine, rows_other))
    all_other = lax.ppermute(all_mine, "core", swap)
    return update(panel, centres_cols, rows_own, rows_other, all_mine, all_other, trailing)


def solution(mesh):
    col_count, row_count = mesh.devices.shape
    chips = col_count // CORES
    fine = Mesh(mesh.devices.reshape(chips, CORES, row_count), ("chip", "core", "row"))

    def step(*arrays):
        return on_device(chips, row_count, *arrays)

    col = ("chip", "core")
    return jax.shard_map(
        step,
        mesh=fine,
        in_specs=(P(), P(col, None), P(("row",) + col, None), P(col, None), P("row", col)),
        out_specs=P("row", col),
        check_vma=False,
    )
```

```python
import math

import jax
import jax.numpy as jnp
from jax import lax
from jax.experimental import pallas as pl
from jax.experimental.pallas import tpu as pltpu
from jax.sharding import Mesh, PartitionSpec as P

LAYERS = 3
CORES = 2
LANES = 128
STEP = 64
WIDE = (0.4999999720071538, -0.06830646500676399, 0.028277340639243406, -0.01566003030791659,
        0.008837209300279753, -0.003820798788545866, 0.0008313362870811599)
NARROW = (0.4999769000530011, -0.06803611787881512, 0.026989768593852003, -0.012483028758839653,
          0.004564983607401579, -0.0008544733222650566)


def repeat_gather(piece, axis, count):
    return lax.all_to_all(jnp.broadcast_to(piece[None], (count,) + piece.shape), axis, 0, 0)


def split(values):
    high = values.astype(jnp.bfloat16)
    return high, (values - high.astype(jnp.float32)).astype(jnp.bfloat16)


def dot_t(left, right):
    return lax.dot_general(left, right, (((1,), (1,)), ((), ())), preferred_element_type=jnp.float32)


def poly(x, coefs):
    total = coefs[-1]
    for coef in coefs[-2::-1]:
        total = total * x + coef
    return total


def layers(rho):
    theta = rho
    for layer in range(LAYERS):
        size = jnp.abs(rho) if layer == 0 else rho
        rest = jnp.maximum(1.0 - size, 1e-30)
        below = rest * lax.rsqrt(rest)
        above = 1.0 + size
        above = above * lax.rsqrt(above) * (1.0 / math.pi)
        angle = below * poly(size, NARROW if layer == 2 else WIDE)
        zero_order = 1.0 - angle
        if layer == 0:
            zero_order = jnp.where(rho < 0.0, angle, zero_order)
        rho_next = below * above + zero_order * rho
        theta = theta * zero_order + rho_next
        rho = rho_next
    return theta


def prep_body(x_hbm, inv_hbm, rows_ref, kept_ref, sent_ref, x_ref, inv_ref, sems):
    row, core = lax.axis_index("row"), lax.axis_index("core")
    size, width = x_ref.shape
    take = pl.ds(pl.multiple_of(row * size, size), size)
    copy_x = pltpu.make_async_copy(x_hbm.at[take, :], x_ref, sems.at[0])
    copy_inv = pltpu.make_async_copy(inv_hbm.at[take, :], inv_ref, sems.at[1])
    copy_x.start()
    copy_inv.start()
    half, groups = width // CORES, inv_ref.shape[1] // LANES
    rows = size // CORES
    base = size * (half // LANES)
    end = base + 2 * rows * groups
    count = rows_ref.shape[0]
    for out_ref in (kept_ref, sent_ref):
        out_ref[end:, :] = jnp.zeros((kept_ref.shape[0] - end, LANES), jnp.bfloat16)
        for which in range(CORES):

            @pl.when(core == which)
            def _():
                for i in range(width // LANES):
                    to = end + CORES * count * i + count * which
                    out_ref[to : to + count, :] = rows_ref[:, LANES * i : LANES * (i + 1)]

    copy_x.wait()
    copy_inv.wait()
    for out_ref, which in ((kept_ref, core), (sent_ref, 1 - core)):
        for i in range(half // LANES):
            at = pl.multiple_of(which * half + LANES * i, LANES)
            out_ref[size * i : size * (i + 1), :] = x_ref[:, pl.ds(at, LANES)]
    for out_ref, which in ((kept_ref, core), (sent_ref, 1 - core)):
        for i in range(groups):
            at = pl.multiple_of(which * rows, rows)
            high, low = split(inv_ref[pl.ds(at, rows), LANES * i : LANES * (i + 1)])
            out_ref[base + rows * i : base + rows * (i + 1), :] = high
            shift = base + rows * groups
            out_ref[shift + rows * i : shift + rows * (i + 1), :] = low


VMEM = pl.BlockSpec(memory_space=pltpu.VMEM)
ANY = pl.BlockSpec(memory_space=pl.ANY)
SMALL = pltpu.CompilerParams(vmem_limit_bytes=4 * 2**20)


def prep(vectors, inverse, rows, quarter):
    size, width = vectors.shape
    total = (width * quarter // CORES + 2 * quarter * size // CORES + CORES * rows.size) // LANES
    out = jax.ShapeDtypeStruct((total, LANES), jnp.bfloat16)
    return pl.pallas_call(
        prep_body,
        in_specs=[ANY, ANY, VMEM],
        out_specs=[VMEM, VMEM],
        out_shape=[out, out],
        scratch_shapes=[
            pltpu.VMEM((quarter, width), jnp.bfloat16),
            pltpu.VMEM((quarter, size), jnp.float32),
            pltpu.SemaphoreType.DMA((2,)),
        ],
        compiler_params=pltpu.CompilerParams(vmem_limit_bytes=211 * 2**18),
        name="prep",
    )(vectors, inverse, rows)


def owner_of(panel_ref):
    blocks = panel_ref.shape[1]
    at = lax.broadcasted_iota(jnp.int32, (1, blocks), 1)
    found = jnp.where(panel_ref[...] == blocks // 4, at, 0).astype(jnp.float32)
    return jnp.sum(found).astype(jnp.int32)


def first_body(panel_ref, kept_ref, got_ref, out_ref, rows_ref):
    total = out_ref.shape[0] * out_ref.shape[1]
    count = rows_ref.shape[0]
    core = lax.axis_index("core")
    kept = owner_of(panel_ref) % CORES == core
    out_ref[...] = jnp.where(kept, kept_ref[:total], got_ref[:total]).reshape(out_ref.shape)
    at = pl.ds(pl.multiple_of(total + core * count, count), count)
    rows_ref[...] = (kept_ref[at, :].astype(jnp.float32) + got_ref[at, :].astype(jnp.float32)).astype(jnp.bfloat16)


def first_operand(panel, kept, got, chips, per_chip):
    count = (kept.shape[0] - chips * per_chip) // CORES
    return pl.pallas_call(
        first_body,
        in_specs=[VMEM, VMEM, VMEM],
        out_specs=[VMEM, VMEM],
        out_shape=[
            jax.ShapeDtypeStruct((chips, per_chip, LANES), jnp.bfloat16),
            jax.ShapeDtypeStruct((count, LANES), jnp.bfloat16),
        ],
        compiler_params=SMALL,
        name="first_operand",
    )(panel, kept, got)


def second_body(panel_ref, came_ref, rows_ref, out_ref):
    chips, per_chip, _ = came_ref.shape
    piece = came_ref[owner_of(panel_ref) // CORES]
    out_ref[:, :per_chip, :] = jnp.broadcast_to(piece[None], (chips, per_chip, LANES))
    out_ref[:, per_chip:, :] = jnp.broadcast_to(rows_ref[...][None], (chips,) + rows_ref.shape)


def second_operand(panel, came, rows):
    chips, per_chip, _ = came.shape
    return pl.pallas_call(
        second_body,
        in_specs=[VMEM, VMEM, VMEM],
        out_specs=VMEM,
        out_shape=jax.ShapeDtypeStruct((chips, per_chip + rows.shape[0], LANES), came.dtype),
        compiler_params=SMALL,
        name="second_operand",
    )(panel, came, rows)


def third_body(came_ref, out_ref):
    per_chip = out_ref.shape[1] // came_ref.shape[0]
    piece = came_ref[:, :per_chip, :].reshape(out_ref.shape[1:])
    for q in range(out_ref.shape[0]):
        out_ref[q] = piece


def third_operand(came, row_count, per_chip):
    return pl.pallas_call(
        third_body,
        in_specs=[VMEM],
        out_specs=VMEM,
        out_shape=jax.ShapeDtypeStruct((row_count, came.shape[0] * per_chip, LANES), came.dtype),
        compiler_params=SMALL,
        name="third_operand",
    )(came)


def triple(ref, rows, at, values, swapped):
    high, low = split(values)
    width = values.shape[1]
    for i, part in enumerate((high, low, high) if swapped else (high, high, low)):
        ref[rows, at + width * i : at + width * (i + 1)] = part


def unpack(got_ref, x_ref, inverse_ref, places):
    quarters = got_ref.shape[0]
    size, half = x_ref.shape
    quarter = size // quarters
    part = quarter // CORES
    groups, inv_groups = half // LANES, size // LANES
    each = inv_groups // 2
    for q in range(quarters):
        for i in range(groups):
            x_ref[quarter * q : quarter * (q + 1), LANES * i : LANES * (i + 1)] = got_ref[q, quarter * i : quarter * (i + 1), :]
        to = places[q]
        for n in range(2):
            for i in range(inv_groups):
                at = quarter * groups + (n * inv_groups + i) * part
                block = got_ref[q, at : at + part, :]
                for place in (0, 2) if n == 0 else (1,):
                    lane = LANES * (inv_groups * place + i)
                    inverse_ref[to : to + part, lane : lane + LANES] = block


def squares(x_ref):
    wide = x_ref[...].astype(jnp.float32)
    total = jnp.sum(wide * wide, axis=1, keepdims=True)
    return jnp.broadcast_to(total, (x_ref.shape[0], LANES)).T[:8]


def half_body(cols_ref, rows_own_ref, rows_other_ref, mine_hbm,
              col_norm_ref, row_norm_ref, gram_cols_ref, gram_rows_ref, square_ref, inverse_ref,
              x_ref, mine_ref, sem):
    copy = pltpu.make_async_copy(mine_hbm, mine_ref, sem)
    copy.start()
    for pieces, to_ref in (((cols_ref,), col_norm_ref), ((rows_own_ref, rows_other_ref), row_norm_ref)):

        @pl.loop(0, to_ref.shape[0] // LANES)
        def _(i):
            at = pl.ds(pl.multiple_of(i * LANES, LANES), LANES)
            total = 1e-06
            for piece_ref in pieces:
                wide = piece_ref[at, :].astype(jnp.float32)
                total += jnp.sum(wide * wide, axis=1, keepdims=True)
            to_ref[at, :] = jnp.broadcast_to(jnp.sqrt(total), (LANES, LANES))

    copy.wait()
    half, count = x_ref.shape[1], inverse_ref.shape[0]
    quarters = mine_ref.shape[0]
    unpack(mine_ref, x_ref, inverse_ref, [count // quarters * q for q in range(quarters)])
    own = pl.ds(pl.multiple_of(lax.axis_index("core") * half, half), half)
    gram_cols_ref[...] = dot_t(cols_ref[:, own], x_ref[...])
    gram_rows_ref[...] = dot_t(rows_own_ref[...], x_ref[...])
    square_ref[...] = squares(x_ref)


def half_step(cols, rows_own, rows_other, mine):
    size, width = cols.shape
    norm = jax.ShapeDtypeStruct((size, LANES), jnp.float32)
    square = jax.ShapeDtypeStruct((size, size), jnp.float32)
    return pl.pallas_call(
        half_body,
        in_specs=[VMEM] * 3 + [pl.BlockSpec(memory_space=pl.ANY)],
        out_specs=[VMEM] * 6,
        out_shape=[
            norm,
            norm,
            square,
            square,
            jax.ShapeDtypeStruct((8, size), jnp.float32),
            jax.ShapeDtypeStruct((size // CORES, 3 * size), jnp.bfloat16),
        ],
        scratch_shapes=[
            pltpu.VMEM((size, width // CORES), jnp.bfloat16),
            pltpu.VMEM(mine.shape, mine.dtype),
            pltpu.SemaphoreType.DMA,
        ],
        compiler_params=pltpu.CompilerParams(vmem_limit_bytes=9 * 2**20),
        cost_estimate=pl.CostEstimate(
            flops=4 * size * size * (width // CORES), bytes_accessed=8 * 2**20, transcendentals=0
        ),
        name="half_step",
    )(cols, rows_own, rows_other, mine)


def update_body(panel_ref, cols_ref, col_norm_ref, rows_ref, row_norm_ref, gram_cols_ref, gram_rows_ref, square_ref,
                inverse_own_ref, other_ref, trailing_ref, out_ref,
                x_ref, inverse_ref, gram_ref, gram_sum_ref, norm_ref, inv_ref, k_cols_ref, k_rows_ref, left_ref, right_ref):
    size, half = x_ref.shape
    core = lax.axis_index("core")
    quarters, count = other_ref.shape[0], inverse_own_ref.shape[0]
    pair, part = count // 2, count // quarters
    unpack(other_ref, x_ref, inverse_ref, [count * (q // 2) + pair + part * (q % 2) for q in range(quarters)])
    for n in range(2):
        inverse_ref[count * n : count * n + pair, :] = inverse_own_ref[pair * n : pair * (n + 1), :]
    norm = jnp.sqrt(square_ref[...] + squares(x_ref) + 1e-06)
    norm_ref[...] = jnp.concatenate([norm] * (STEP // 8), axis=0)
    inv_ref[...] = jnp.concatenate([1.0 / norm] * (STEP // 8), axis=0)

    def values_of(gram, from_norm, to_ref, at):
        norm = jnp.concatenate([from_norm] * (size // LANES), axis=1)
        cosine = gram * (1.0 / norm) * inv_ref[...]
        values = layers(jnp.clip(cosine, -1.0, 1.0)) * (norm * norm_ref[...])
        triple(to_ref, at, 0, values, False)

    theirs = pl.ds(pl.multiple_of((1 - core) * half, half), half)
    gram_ref[...] = gram_cols_ref[...] + dot_t(cols_ref[:, theirs], x_ref[...])
    n_steps = size // STEP

    def block(i, extent):
        return pl.ds(pl.multiple_of(i * extent, extent), extent)

    gram_sum_ref[...] = gram_rows_ref[...] + dot_t(rows_ref[...], x_ref[...])

    for gram, from_norm, k_ref, to_ref, swapped in (
        (gram_ref, col_norm_ref, k_cols_ref, right_ref, True),
        (gram_sum_ref, row_norm_ref, k_rows_ref, left_ref, False),
    ):

        @pl.loop(0, n_steps)
        def _(i):
            at = block(i, STEP)
            values_of(gram[at, :], from_norm[at, :], k_ref, at)

        triple(to_ref, slice(0, size), 0, dot_t(k_ref[...], inverse_ref[...]), swapped)

    blocks = panel_ref.shape[1]
    here = lax.broadcasted_iota(jnp.int32, (1, blocks), 1) == CORES * lax.axis_index("chip") + core
    own_rank = jnp.sum(jnp.where(here, panel_ref[...], 0).astype(jnp.float32))
    old = trailing_ref[...]
    out_ref[...] = jnp.where(own_rank > blocks // 4, old - dot_t(left_ref[...], right_ref[...]), old)


def update(panel, cols, rows_own, rows_other, mine, other, trailing):
    size, width = cols.shape
    col_norm, row_norm, gram_cols, gram_rows, square, inverse_own = half_step(cols, rows_own, rows_other, mine)
    thrice = pltpu.VMEM((size, 3 * size), jnp.bfloat16)
    lanes = pltpu.VMEM((STEP, size), jnp.float32)
    return pl.pallas_call(
        update_body,
        in_specs=[VMEM] * 11,
        out_specs=VMEM,
        out_shape=jax.ShapeDtypeStruct(trailing.shape, trailing.dtype),
        scratch_shapes=[pltpu.VMEM((size, width // CORES), jnp.bfloat16), thrice]
        + [pltpu.VMEM((size, size), jnp.float32)] * 2
        + [lanes] * 2
        + [thrice] * 4,
        compiler_params=pltpu.CompilerParams(vmem_limit_bytes=22 * 2**20),
        name="update",
    )(panel, cols, col_norm, rows_other, row_norm, gram_cols, gram_rows, square, inverse_own,
      other, trailing)


def on_device(chips, row_count, panel, centres_cols, centres_rows, diag_inverse, trailing):
    size, width = centres_cols.shape
    quarter = size // row_count
    panel = panel[None]
    swap = [(0, 1), (1, 0)]

    kept, sent = prep(centres_cols, diag_inverse, centres_rows, quarter)
    got = lax.ppermute(sent, "core", swap)
    per_chip = (2 * width * quarter // CORES) // (LANES * chips)
    outgoing, rows_chip = first_operand(panel, kept, got, chips, per_chip)
    first = lax.all_to_all(outgoing, "chip", 0, 0)
    second = lax.all_to_all(second_operand(panel, first, rows_chip), "chip", 0, 0)
    all_mine = lax.all_to_all(third_operand(second, row_count, per_chip), "row", 0, 0)

    tiles = [second[:, i : i + 8] for i in range(per_chip, second.shape[1], 8)]
    rows_own = jnp.concatenate([tile.reshape(size, LANES) for tile in tiles], axis=1)
    rows_other = lax.ppermute(rows_own, "core", swap)
    all_mine, rows_other = lax.optimization_barrier((all_mine, rows_other))
    all_other = lax.ppermute(all_mine, "core", swap)
    return update(panel, centres_cols, rows_own, rows_other, all_mine, all_other, trailing)


def solution(mesh):
    col_count, row_count = mesh.devices.shape
    chips = col_count // CORES
    fine = Mesh(mesh.devices.reshape(chips, CORES, row_count), ("chip", "core", "row"))

    def step(*arrays):
        return on_device(chips, row_count, *arrays)

    col = ("chip", "core")
    return jax.shard_map(
        step,
        mesh=fine,
        in_specs=(P(), P(col, None), P(("row",) + col, None), P(col, None), P("row", col)),
        out_specs=P("row", col),
        check_vma=False,
    )
```

```python
import math

import jax
import jax.numpy as jnp
from jax import lax
from jax.experimental import pallas as pl
from jax.experimental.pallas import tpu as pltpu
from jax.sharding import Mesh, PartitionSpec as P

LAYERS = 3
CORES = 2
LANES = 128
STEP = 64
WIDE = (0.4999999720071538, -0.06830646500676399, 0.028277340639243406, -0.01566003030791659,
        0.008837209300279753, -0.003820798788545866, 0.0008313362870811599)
NARROW = (0.4999769000530011, -0.06803611787881512, 0.026989768593852003, -0.012483028758839653,
          0.004564983607401579, -0.0008544733222650566)


def repeat_gather(piece, axis, count):
    return lax.all_to_all(jnp.broadcast_to(piece[None], (count,) + piece.shape), axis, 0, 0)


def split(values):
    high = values.astype(jnp.bfloat16)
    return high, (values - high.astype(jnp.float32)).astype(jnp.bfloat16)


def dot_t(left, right):
    return lax.dot_general(left, right, (((1,), (1,)), ((), ())), preferred_element_type=jnp.float32)


def poly(x, coefs):
    total = coefs[-1]
    for coef in coefs[-2::-1]:
        total = total * x + coef
    return total


def layers(rho):
    theta = rho
    for layer in range(LAYERS):
        size = jnp.abs(rho) if layer == 0 else rho
        rest = jnp.maximum(1.0 - size, 1e-30)
        below = rest * lax.rsqrt(rest)
        above = 1.0 + size
        above = above * lax.rsqrt(above) * (1.0 / math.pi)
        angle = below * poly(size, NARROW if layer == 2 else WIDE)
        zero_order = 1.0 - angle
        if layer == 0:
            zero_order = jnp.where(rho < 0.0, angle, zero_order)
        rho_next = below * above + zero_order * rho
        theta = theta * zero_order + rho_next
        rho = rho_next
    return theta


def prep_body(x_hbm, inv_hbm, rows_hbm, panel_hbm, kept_ref, sent_ref, panel_ref, x_ref, inv_ref, rows_ref, sems):
    row, core = lax.axis_index("row"), lax.axis_index("core")
    size, width = x_ref.shape
    take = pl.ds(pl.multiple_of(row * size, size), size)
    copy_x = pltpu.make_async_copy(x_hbm.at[take, :], x_ref, sems.at[0])
    copy_inv = pltpu.make_async_copy(inv_hbm.at[take, :], inv_ref, sems.at[1])
    copy_rows = pltpu.make_async_copy(rows_hbm, rows_ref, sems.at[2])
    copy_panel = pltpu.make_async_copy(panel_hbm, panel_ref, sems.at[3])
    copy_rows.start()
    copy_panel.start()
    copy_x.start()
    copy_inv.start()
    copy_rows.wait()
    half, groups = width // CORES, inv_ref.shape[1] // LANES
    rows = size // CORES
    base = size * (half // LANES)
    end = base + 2 * rows * groups
    count = rows_ref.shape[0]
    for out_ref in (kept_ref, sent_ref):
        out_ref[end:, :] = jnp.zeros((kept_ref.shape[0] - end, LANES), jnp.bfloat16)
        for which in range(CORES):

            @pl.when(core == which)
            def _():
                for i in range(width // LANES):
                    to = end + CORES * count * i + count * which
                    out_ref[to : to + count, :] = rows_ref[:, LANES * i : LANES * (i + 1)]

    copy_x.wait()
    copy_inv.wait()
    copy_panel.wait()
    for out_ref, which in ((kept_ref, core), (sent_ref, 1 - core)):
        for i in range(half // LANES):
            at = pl.multiple_of(which * half + LANES * i, LANES)
            out_ref[size * i : size * (i + 1), :] = x_ref[:, pl.ds(at, LANES)]
    for out_ref, which in ((kept_ref, core), (sent_ref, 1 - core)):
        for i in range(groups):
            at = pl.multiple_of(which * rows, rows)
            high, low = split(inv_ref[pl.ds(at, rows), LANES * i : LANES * (i + 1)])
            out_ref[base + rows * i : base + rows * (i + 1), :] = high
            shift = base + rows * groups
            out_ref[shift + rows * i : shift + rows * (i + 1), :] = low


VMEM = pl.BlockSpec(memory_space=pltpu.VMEM)
ANY = pl.BlockSpec(memory_space=pl.ANY)
SMALL = pltpu.CompilerParams(vmem_limit_bytes=4 * 2**20)


def prep(panel, vectors, inverse, rows, quarter):
    size, width = vectors.shape
    total = (width * quarter // CORES + 2 * quarter * size // CORES + CORES * rows.size) // LANES
    out = jax.ShapeDtypeStruct((total, LANES), jnp.bfloat16)
    return pl.pallas_call(
        prep_body,
        in_specs=[ANY] * 4,
        out_specs=[VMEM] * 3,
        out_shape=[out, out, jax.ShapeDtypeStruct(panel.shape, panel.dtype)],
        scratch_shapes=[
            pltpu.VMEM((quarter, width), jnp.bfloat16),
            pltpu.VMEM((quarter, size), jnp.float32),
            pltpu.VMEM(rows.shape, rows.dtype),
            pltpu.SemaphoreType.DMA((4,)),
        ],
        compiler_params=pltpu.CompilerParams(vmem_limit_bytes=211 * 2**18),
        name="prep",
    )(vectors, inverse, rows, panel)


def owner_of(panel_ref):
    blocks = panel_ref.shape[1]
    at = lax.broadcasted_iota(jnp.int32, (1, blocks), 1)
    found = jnp.where(panel_ref[...] == blocks // 4, at, 0).astype(jnp.float32)
    return jnp.sum(found).astype(jnp.int32)


def first_body(panel_ref, kept_ref, got_ref, out_ref, rows_ref):
    total = out_ref.shape[0] * out_ref.shape[1]
    count = rows_ref.shape[0]
    core = lax.axis_index("core")
    kept = owner_of(panel_ref) % CORES == core
    out_ref[...] = jnp.where(kept, kept_ref[:total], got_ref[:total]).reshape(out_ref.shape)
    at = pl.ds(pl.multiple_of(total + core * count, count), count)
    rows_ref[...] = (kept_ref[at, :].astype(jnp.float32) + got_ref[at, :].astype(jnp.float32)).astype(jnp.bfloat16)


def first_operand(panel, kept, got, chips, per_chip):
    count = (kept.shape[0] - chips * per_chip) // CORES
    return pl.pallas_call(
        first_body,
        in_specs=[VMEM, VMEM, VMEM],
        out_specs=[VMEM, VMEM],
        out_shape=[
            jax.ShapeDtypeStruct((chips, per_chip, LANES), jnp.bfloat16),
            jax.ShapeDtypeStruct((count, LANES), jnp.bfloat16),
        ],
        compiler_params=SMALL,
        name="first_operand",
    )(panel, kept, got)


def second_body(panel_ref, came_ref, rows_ref, out_ref):
    chips, per_chip, _ = came_ref.shape
    piece = came_ref[owner_of(panel_ref) // CORES]
    out_ref[:, :per_chip, :] = jnp.broadcast_to(piece[None], (chips, per_chip, LANES))
    out_ref[:, per_chip:, :] = jnp.broadcast_to(rows_ref[...][None], (chips,) + rows_ref.shape)


def second_operand(panel, came, rows):
    chips, per_chip, _ = came.shape
    return pl.pallas_call(
        second_body,
        in_specs=[VMEM, VMEM, VMEM],
        out_specs=VMEM,
        out_shape=jax.ShapeDtypeStruct((chips, per_chip + rows.shape[0], LANES), came.dtype),
        compiler_params=SMALL,
        name="second_operand",
    )(panel, came, rows)


def third_body(came_ref, out_ref):
    per_chip = out_ref.shape[1] // came_ref.shape[0]
    piece = came_ref[:, :per_chip, :].reshape(out_ref.shape[1:])
    for q in range(out_ref.shape[0]):
        out_ref[q] = piece


def third_operand(came, row_count, per_chip):
    return pl.pallas_call(
        third_body,
        in_specs=[VMEM],
        out_specs=VMEM,
        out_shape=jax.ShapeDtypeStruct((row_count, came.shape[0] * per_chip, LANES), came.dtype),
        compiler_params=SMALL,
        name="third_operand",
    )(came)


def triple(ref, rows, at, values, swapped):
    high, low = split(values)
    width = values.shape[1]
    for i, part in enumerate((high, low, high) if swapped else (high, high, low)):
        ref[rows, at + width * i : at + width * (i + 1)] = part


def unpack(got_ref, x_ref, inverse_ref, places):
    quarters = got_ref.shape[0]
    size, half = x_ref.shape
    quarter = size // quarters
    part = quarter // CORES
    groups, inv_groups = half // LANES, size // LANES
    each = inv_groups // 2
    for q in range(quarters):
        for i in range(groups):
            x_ref[quarter * q : quarter * (q + 1), LANES * i : LANES * (i + 1)] = got_ref[q, quarter * i : quarter * (i + 1), :]
        to = places[q]
        for n in range(2):
            for i in range(inv_groups):
                at = quarter * groups + (n * inv_groups + i) * part
                block = got_ref[q, at : at + part, :]
                for place in (0, 2) if n == 0 else (1,):
                    lane = LANES * (inv_groups * place + i)
                    inverse_ref[to : to + part, lane : lane + LANES] = block


def squares(x_ref):
    wide = x_ref[...].astype(jnp.float32)
    total = jnp.sum(wide * wide, axis=1, keepdims=True)
    return jnp.broadcast_to(total, (x_ref.shape[0], LANES)).T[:8]


def half_body(cols_ref, rows_own_ref, rows_other_ref, mine_hbm,
              col_norm_ref, row_norm_ref, gram_cols_ref, gram_rows_ref, square_ref, inverse_ref,
              x_ref, mine_ref, sem):
    copy = pltpu.make_async_copy(mine_hbm, mine_ref, sem)
    copy.start()
    for pieces, to_ref in (((cols_ref,), col_norm_ref), ((rows_own_ref, rows_other_ref), row_norm_ref)):

        @pl.loop(0, to_ref.shape[0] // LANES)
        def _(i):
            at = pl.ds(pl.multiple_of(i * LANES, LANES), LANES)
            total = 1e-06
            for piece_ref in pieces:
                wide = piece_ref[at, :].astype(jnp.float32)
                total += jnp.sum(wide * wide, axis=1, keepdims=True)
            to_ref[at, :] = jnp.broadcast_to(jnp.sqrt(total), (LANES, LANES))

    copy.wait()
    half, count = x_ref.shape[1], inverse_ref.shape[0]
    quarters = mine_ref.shape[0]
    unpack(mine_ref, x_ref, inverse_ref, [count // quarters * q for q in range(quarters)])
    own = pl.ds(pl.multiple_of(lax.axis_index("core") * half, half), half)
    gram_cols_ref[...] = dot_t(cols_ref[:, own], x_ref[...])
    gram_rows_ref[...] = dot_t(rows_own_ref[...], x_ref[...])
    square_ref[...] = squares(x_ref)


def half_step(cols, rows_own, rows_other, mine):
    size, width = cols.shape
    norm = jax.ShapeDtypeStruct((size, LANES), jnp.float32)
    square = jax.ShapeDtypeStruct((size, size), jnp.float32)
    return pl.pallas_call(
        half_body,
        in_specs=[VMEM] * 3 + [pl.BlockSpec(memory_space=pl.ANY)],
        out_specs=[VMEM] * 6,
        out_shape=[
            norm,
            norm,
            square,
            square,
            jax.ShapeDtypeStruct((8, size), jnp.float32),
            jax.ShapeDtypeStruct((size // CORES, 3 * size), jnp.bfloat16),
        ],
        scratch_shapes=[
            pltpu.VMEM((size, width // CORES), jnp.bfloat16),
            pltpu.VMEM(mine.shape, mine.dtype),
            pltpu.SemaphoreType.DMA,
        ],
        compiler_params=pltpu.CompilerParams(vmem_limit_bytes=9 * 2**20),
        cost_estimate=pl.CostEstimate(
            flops=4 * size * size * (width // CORES), bytes_accessed=8 * 2**20, transcendentals=0
        ),
        name="half_step",
    )(cols, rows_own, rows_other, mine)


def update_body(panel_ref, cols_ref, col_norm_ref, rows_ref, row_norm_ref, gram_cols_ref, gram_rows_ref, square_ref,
                inverse_own_ref, other_ref, trailing_ref, out_ref,
                x_ref, inverse_ref, gram_ref, gram_sum_ref, norm_ref, inv_ref, k_cols_ref, k_rows_ref, left_ref, right_ref):
    size, half = x_ref.shape
    core = lax.axis_index("core")
    quarters, count = other_ref.shape[0], inverse_own_ref.shape[0]
    pair, part = count // 2, count // quarters
    unpack(other_ref, x_ref, inverse_ref, [count * (q // 2) + pair + part * (q % 2) for q in range(quarters)])
    for n in range(2):
        inverse_ref[count * n : count * n + pair, :] = inverse_own_ref[pair * n : pair * (n + 1), :]
    norm = jnp.sqrt(square_ref[...] + squares(x_ref) + 1e-06)
    norm_ref[...] = jnp.concatenate([norm] * (STEP // 8), axis=0)
    inv_ref[...] = jnp.concatenate([1.0 / norm] * (STEP // 8), axis=0)

    def values_of(gram, from_norm, to_ref, at):
        norm = jnp.concatenate([from_norm] * (size // LANES), axis=1)
        cosine = gram * (1.0 / norm) * inv_ref[...]
        values = layers(jnp.clip(cosine, -1.0, 1.0)) * (norm * norm_ref[...])
        triple(to_ref, at, 0, values, False)

    theirs = pl.ds(pl.multiple_of((1 - core) * half, half), half)
    gram_ref[...] = gram_cols_ref[...] + dot_t(cols_ref[:, theirs], x_ref[...])
    n_steps = size // STEP

    def block(i, extent):
        return pl.ds(pl.multiple_of(i * extent, extent), extent)

    gram_sum_ref[...] = gram_rows_ref[...] + dot_t(rows_ref[...], x_ref[...])

    for gram, from_norm, k_ref, to_ref, swapped in (
        (gram_ref, col_norm_ref, k_cols_ref, right_ref, True),
        (gram_sum_ref, row_norm_ref, k_rows_ref, left_ref, False),
    ):

        @pl.loop(0, n_steps)
        def _(i):
            at = block(i, STEP)
            values_of(gram[at, :], from_norm[at, :], k_ref, at)

        triple(to_ref, slice(0, size), 0, dot_t(k_ref[...], inverse_ref[...]), swapped)

    blocks = panel_ref.shape[1]
    here = lax.broadcasted_iota(jnp.int32, (1, blocks), 1) == CORES * lax.axis_index("chip") + core
    own_rank = jnp.sum(jnp.where(here, panel_ref[...], 0).astype(jnp.float32))
    old = trailing_ref[...]
    out_ref[...] = jnp.where(own_rank > blocks // 4, old - dot_t(left_ref[...], right_ref[...]), old)


def update(panel, cols, rows_own, rows_other, mine, other, trailing):
    size, width = cols.shape
    col_norm, row_norm, gram_cols, gram_rows, square, inverse_own = half_step(cols, rows_own, rows_other, mine)
    thrice = pltpu.VMEM((size, 3 * size), jnp.bfloat16)
    lanes = pltpu.VMEM((STEP, size), jnp.float32)
    return pl.pallas_call(
        update_body,
        in_specs=[VMEM] * 11,
        out_specs=VMEM,
        out_shape=jax.ShapeDtypeStruct(trailing.shape, trailing.dtype),
        scratch_shapes=[pltpu.VMEM((size, width // CORES), jnp.bfloat16), thrice]
        + [pltpu.VMEM((size, size), jnp.float32)] * 2
        + [lanes] * 2
        + [thrice] * 4,
        compiler_params=pltpu.CompilerParams(vmem_limit_bytes=22 * 2**20),
        name="update",
    )(panel, cols, col_norm, rows_other, row_norm, gram_cols, gram_rows, square, inverse_own,
      other, trailing)


def on_device(chips, row_count, panel, centres_cols, centres_rows, diag_inverse, trailing):
    size, width = centres_cols.shape
    quarter = size // row_count
    panel = panel[None]
    swap = [(0, 1), (1, 0)]

    kept, sent, panel = prep(panel, centres_cols, diag_inverse, centres_rows, quarter)
    got = lax.ppermute(sent, "core", swap)
    per_chip = (2 * width * quarter // CORES) // (LANES * chips)
    outgoing, rows_chip = first_operand(panel, kept, got, chips, per_chip)
    first = lax.all_to_all(outgoing, "chip", 0, 0)
    second = lax.all_to_all(second_operand(panel, first, rows_chip), "chip", 0, 0)
    all_mine = lax.all_to_all(third_operand(second, row_count, per_chip), "row", 0, 0)

    tiles = [second[:, i : i + 8] for i in range(per_chip, second.shape[1], 8)]
    rows_own = jnp.concatenate([tile.reshape(size, LANES) for tile in tiles], axis=1)
    rows_other = lax.ppermute(rows_own, "core", swap)
    all_mine, rows_other = lax.optimization_barrier((all_mine, rows_other))
    all_other = lax.ppermute(all_mine, "core", swap)
    return update(panel, centres_cols, rows_own, rows_other, all_mine, all_other, trailing)


def solution(mesh):
    col_count, row_count = mesh.devices.shape
    chips = col_count // CORES
    fine = Mesh(mesh.devices.reshape(chips, CORES, row_count), ("chip", "core", "row"))

    def step(*arrays):
        return on_device(chips, row_count, *arrays)

    col = ("chip", "core")
    return jax.shard_map(
        step,
        mesh=fine,
        in_specs=(P(), P(col, None), P(("row",) + col, None), P(col, None), P("row", col)),
        out_specs=P("row", col),
        check_vma=False,
    )
```
